32 devices in a mesh: dp: 8 (over y, x, core), tensor: 4 (over z).
Axes of the slice: x: 2, y: 2, z: 4, core: 2. Of those that a mesh axis runs over, the one named last changes fastest.
Arguments:
- block_input: bfloat16 [8192, 1024], P(('dp', 'tensor')), may hold values from -24 to 24
- lengths: int32 [8], P('dp'), may hold values from 128 to 1024, as said below
- query_weight: bfloat16 [1024, 1024], P('dp', 'tensor'), may hold values from -0.1875 to 0.1875
- key_weight: bfloat16 [1024, 1024], P('dp', 'tensor'), may hold values from -0.1875 to 0.1875
- value_weight: bfloat16 [1024, 1024], P('dp', 'tensor'), may hold values from -0.1875 to 0.1875
- query_bias: bfloat16 [1024], P(('tensor', 'dp')), may hold values from -4 to 4
- value_bias: bfloat16 [1024], P(('tensor', 'dp')), may hold values from -4 to 4
- output_weight: bfloat16 [1024, 1024], P('tensor', 'dp'), may hold values from -0.75 to 0.75
- output_bias: float32 [1024], P(('dp', 'tensor')), may hold values from -4 to 4
- first_gain: float32 [1024], P(('dp', 'tensor')), may hold values from 0.1 to 1.9
- first_shift: float32 [1024], P(('dp', 'tensor')), may hold values from -3 to 3
- inner_weight: bfloat16 [1024, 4096], P('dp', 'tensor'), may hold values from -0.1875 to 0.1875
- inner_bias: bfloat16 [4096], P(('tensor', 'dp')), may hold values from -3 to 3
- outer_weight: bfloat16 [4096, 1024], P('tensor', 'dp'), may hold values from -0.09375 to 0.09375
- outer_bias: float32 [1024], P(('dp', 'tensor')), may hold values from -4 to 4
- second_gain: float32 [1024], P(('dp', 'tensor')), may hold values from 0.1 to 1.9
- second_shift: float32 [1024], P(('dp', 'tensor')), may hold values from -3 to 3
- cotangent: bfloat16 [8192, 1024], P(('dp', 'tensor')), may hold values from -6 to 6
Outputs:
- block_output: bfloat16 [8192, 1024], P(('dp', 'tensor'))
- input_grad: float32 [8192, 1024], P(('dp', 'tensor'))
- query_weight_grad: float32 [1024, 1024], P('dp', 'tensor')
- key_weight_grad: float32 [1024, 1024], P('dp', 'tensor')
- value_weight_grad: float32 [1024, 1024], P('dp', 'tensor')
- query_bias_grad: float32 [1024], P(('tensor', 'dp'))
- value_bias_grad: float32 [1024], P(('tensor', 'dp'))
- output_weight_grad: float32 [1024, 1024], P('tensor', 'dp')
- output_bias_grad: float32 [1024], P(('dp', 'tensor'))
- first_gain_grad: float32 [1024], P(('dp', 'tensor'))
- first_shift_grad: float32 [1024], P(('dp', 'tensor'))
- inner_weight_grad: float32 [1024, 4096], P('dp', 'tensor')
- inner_bias_grad: float32 [4096], P(('tensor', 'dp'))
- outer_weight_grad: float32 [4096, 1024], P('tensor', 'dp')
- outer_bias_grad: float32 [1024], P(('dp', 'tensor'))
- second_gain_grad: float32 [1024], P(('dp', 'tensor'))
- second_shift_grad: float32 [1024], P(('dp', 'tensor'))
The draws below stay inside these ranges and needn't reach their ends.
Inputs may be any that keep to these rules, and one draw needn't show every extreme that they name: lengths[s] tokens at the start of sequence s are valid keys; one sequence is full and one has the fewest.
All inputs are finite; a program needn't handle non-finite values.
Results may differ from the reference program's by a relative error of at most 0.009.
The reference program's roundings to bfloat16 on the way count: a program that leaves them out, or rounds other values in their place, can miss the bound.
Values may be sent and summed in bfloat16 or wider, within the bound.
A program may use at most 128 MiB of HBM per device.

```python
import math
import jax
import jax.numpy as jnp
from jax import lax

D = 1024
HEADS = 16
HEAD_DIM = 64
FF = 4096
SEQ_LEN = 1024
SEQUENCES = 8
TOKENS = 8192


def draw_block_input(key, part):
    key_base, key_scale = jax.random.split(key)
    base_draw = jnp.clip(jax.random.normal(key_base, (TOKENS, D), jnp.float32), -6.0, 6.0)
    top_log = math.log(3.0)
    row_scale = jnp.exp(jax.random.uniform(key_scale, (TOKENS, 1), jnp.float32, 0.0, top_log))
    return (base_draw * row_scale).astype(jnp.bfloat16)


def draw_lengths(key, part):
    key_len, key_pick = jax.random.split(key)
    drawn_len = jax.random.randint(key_len, (SEQUENCES,), SEQ_LEN // 8, SEQ_LEN + 1)
    picked = jax.random.permutation(key_pick, SEQUENCES)
    drawn_len = drawn_len.at[picked[0]].set(SEQ_LEN)
    drawn_len = drawn_len.at[picked[1]].set(SEQ_LEN // 8)
    return drawn_len.astype(jnp.int32)


def raised(result, stream_key, source, target, shards_of, factor):
    def block_of(position):
        return (jnp.arange(result.shape[position]) // (result.shape[position] // shards_of)).reshape((-1,) + (1,) * (result.ndim - 1 - position))

    one_side = jax.random.permutation(stream_key, shards_of)[block_of(target)]
    far = (block_of(target) + shards_of // 2) % shards_of
    return jnp.where((block_of(source) == one_side) | (block_of(source) == far), factor * result, result)


def shard_levels(rng, extent, cuts, smallest, top_value):
    factor_of = 1.0
    for dim, shards_of in cuts:
        heights = jax.random.uniform(jax.random.fold_in(jax.random.fold_in(rng, 6), dim), (shards_of,), jnp.float32, smallest / len(cuts), top_value / len(cuts))
        factor_of = factor_of * jnp.repeat(jnp.exp(heights), extent[dim] // shards_of).reshape((-1,) + (1,) * (len(extent) - 1 - dim))
    return factor_of


def scatter_about(key, shape, width, limit, cuts=(), dtype=jnp.bfloat16):
    result = width * jax.random.normal(key, shape, jnp.float32)
    if cuts:
        result = result * shard_levels(key, shape, cuts, -0.22, 0.18)
    return jnp.clip(result, -limit, limit).astype(dtype)


def gaussian_with(key, shape, deviation, bound, cuts, heavy, held_as=jnp.bfloat16):
    values = deviation * jax.random.normal(key, shape, jnp.float32)
    if cuts:
        values = values * shard_levels(key, shape, cuts, -0.22, 0.18)
    return jnp.clip(raised(values, jax.random.fold_in(key, 3), *heavy), -bound, bound).astype(held_as)


def setup_inputs(seed: int = 0) -> dict:
    arg_keys = jax.random.split(jax.random.key(seed), 19)
    block_input = draw_block_input(jax.random.fold_in(arg_keys[18], 71), 0)
    lengths = draw_lengths(jax.random.fold_in(arg_keys[18], 71), 0)
    query_weight = scatter_about(arg_keys[2], (D, D), D ** -0.5, 0.1875, ((0, 8), (1, 4)))
    key_weight = scatter_about(arg_keys[3], (D, D), D ** -0.5, 0.1875, ((0, 8), (1, 4)))
    value_weight = scatter_about(arg_keys[4], (D, D), D ** -0.5, 0.1875, ((0, 8), (1, 4)))
    query_bias = scatter_about(arg_keys[5], (D,), 1.0, 4.0, ((0, 32),))
    value_bias = scatter_about(arg_keys[6], (D,), 1.0, 4.0, ((0, 32),))
    output_weight = scatter_about(arg_keys[7], (D, D), (D // 16) ** -0.5, 0.75, ((0, 4), (1, 8)))
    output_bias = scatter_about(arg_keys[8], (D,), 1.0, 4.0, ((0, 32),), jnp.float32)
    first_gain = jnp.clip(1.0 + 0.18 * jax.random.normal(arg_keys[9], (D,), jnp.float32), 0.1, 1.9)
    first_shift = scatter_about(arg_keys[10], (D,), 0.5, 3.0, ((0, 32),), jnp.float32)
    inner_weight = scatter_about(arg_keys[11], (D, FF), D ** -0.5, 0.1875, ((0, 8), (1, 4)))
    inner_bias = scatter_about(arg_keys[12], (FF,), 0.5, 3.0, ((0, 32),))
    outer_weight = scatter_about(arg_keys[13], (FF, D), FF ** -0.5, 0.09375, ((0, 4), (1, 8)))
    outer_bias = scatter_about(arg_keys[14], (D,), 1.0, 4.0, ((0, 32),), jnp.float32)
    second_gain = jnp.clip(1.0 + 0.18 * jax.random.normal(arg_keys[15], (D,), jnp.float32), 0.1, 1.9)
    second_shift = scatter_about(arg_keys[16], (D,), 0.5, 3.0, ((0, 32),), jnp.float32)
    cotangent = gaussian_with(arg_keys[17], (TOKENS, D), 1.0, 6.0, ((0, 32),), (0, 1, 32, 2.75))
    return {"block_input": block_input, "lengths": lengths, "query_weight": query_weight, "key_weight": key_weight, "value_weight": value_weight, "query_bias": query_bias, "value_bias": value_bias, "output_weight": output_weight, "output_bias": output_bias, "first_gain": first_gain, "first_shift": first_shift, "inner_weight": inner_weight, "inner_bias": inner_bias, "outer_weight": outer_weight, "outer_bias": outer_bias, "second_gain": second_gain, "second_shift": second_shift, "cotangent": cotangent}


inv_root2 = 0.7071067811865476
inv_root2pi = 0.3989422804014327
norm_eps = 1e-06

def gelu_cdf(values):
    return 0.5 * (1.0 + jax.scipy.special.erf(values * inv_root2))

def row_norm(resid_rows, norm_gain, norm_shift):
    center = resid_rows - lax.optimization_barrier(jnp.mean(resid_rows, axis=-1, keepdims=True))
    inverse = lax.rsqrt(lax.optimization_barrier(jnp.mean(center * center, axis=-1, keepdims=True)) + norm_eps)
    return center * inverse * norm_gain + norm_shift

def norm_back(resid_rows, norm_gain, upstream):
    center = resid_rows - lax.optimization_barrier(jnp.mean(resid_rows, axis=-1, keepdims=True))
    inverse = lax.rsqrt(lax.optimization_barrier(jnp.mean(center * center, axis=-1, keepdims=True)) + norm_eps)
    normed = center * inverse
    scaled_up = upstream * norm_gain
    d_resid = inverse * (scaled_up - lax.optimization_barrier(jnp.mean(scaled_up, axis=-1, keepdims=True)) - normed * lax.optimization_barrier(jnp.mean(scaled_up * normed, axis=-1, keepdims=True)))
    return (d_resid, lax.optimization_barrier(jnp.sum(upstream * normed, axis=0)), lax.optimization_barrier(jnp.sum(upstream, axis=0)))

def round_keep(values):
    return lax.optimization_barrier(values.astype(jnp.bfloat16))

def dense(left, right):
    return jnp.dot(left, right, preferred_element_type=jnp.float32)

def split_heads(matrix):
    return matrix.reshape(SEQ_LEN, HEADS, HEAD_DIM).astype(jnp.float32)

def reference(block_input, lengths, query_weight, key_weight, value_weight, query_bias, value_bias, output_weight, output_bias, first_gain, first_shift, inner_weight, inner_bias, outer_weight, outer_bias, second_gain, second_shift, cotangent):
    scale_qk = HEAD_DIM ** (-0.5)

    def one_sequence(totals, pieces):
        seq_rows, upstream, length = pieces
        q_rows = round_keep(dense(seq_rows, query_weight) + query_bias.astype(jnp.float32))
        k_rows = round_keep(dense(seq_rows, key_weight))
        v_rows = round_keep(dense(seq_rows, value_weight) + value_bias.astype(jnp.float32))
        q_heads = split_heads(q_rows)
        k_heads = split_heads(k_rows)
        v_heads = split_heads(v_rows)
        key_valid = jnp.arange(SEQ_LEN) < length
        scores = jnp.einsum('qhd,khd->hqk', q_heads, k_heads) * scale_qk
        scores = jnp.where(key_valid[None, None, :], scores, -jnp.inf)
        row_top = lax.optimization_barrier(jnp.max(scores, axis=-1, keepdims=True))
        log_total = row_top + jnp.log(lax.optimization_barrier(jnp.sum(jnp.exp(scores - row_top), axis=-1, keepdims=True)))
        attn_probs = jnp.exp(scores - log_total)
        probs_b = round_keep(attn_probs).astype(jnp.float32)
        context = round_keep(jnp.einsum('hqk,khd->qhd', probs_b, v_heads).reshape(SEQ_LEN, D))
        resid_one = seq_rows.astype(jnp.float32) + dense(context, output_weight) + output_bias
        middle = row_norm(resid_one, first_gain, first_shift)
        middle_b = round_keep(middle)
        pre_act = dense(middle_b, inner_weight) + inner_bias.astype(jnp.float32)
        hidden_b = round_keep(pre_act * gelu_cdf(pre_act))
        resid_two = middle + dense(hidden_b, outer_weight) + outer_bias
        block_out = row_norm(resid_two, second_gain, second_shift).astype(jnp.bfloat16)
        d_resid2, gain2_grad, shift2_grad = norm_back(resid_two, second_gain, upstream.astype(jnp.float32))
        d_ffn = round_keep(d_resid2)
        outer_grad = dense(hidden_b.T, d_ffn)
        gelu_slope = gelu_cdf(pre_act) + pre_act * inv_root2pi * jnp.exp(-0.5 * pre_act * pre_act)
        d_pre = dense(d_ffn, outer_weight.T) * gelu_slope
        d_pre_b = round_keep(d_pre)
        inner_grad = dense(middle_b.T, d_pre_b)
        d_middle = dense(d_pre_b, inner_weight.T) + d_resid2
        d_resid1, gain1_grad, shift1_grad = norm_back(resid_one, first_gain, d_middle)
        d_attn = round_keep(d_resid1)
        output_grad = dense(context.T, d_attn)
        d_context = round_keep(dense(d_attn, output_weight.T))
        d_ctx_heads = split_heads(d_context)
        d_probs = jnp.einsum('qhd,khd->hqk', d_ctx_heads, v_heads)
        row_inner = lax.optimization_barrier(jnp.sum(attn_probs * d_probs, axis=-1, keepdims=True))
        d_scores = round_keep(attn_probs * (d_probs - row_inner) * scale_qk).astype(jnp.float32)
        d_query = jnp.einsum('hqk,khd->qhd', d_scores, k_heads).reshape(SEQ_LEN, D)
        d_key = jnp.einsum('hqk,qhd->khd', d_scores, q_heads).reshape(SEQ_LEN, D)
        d_value = jnp.einsum('hqk,qhd->khd', probs_b, d_ctx_heads).reshape(SEQ_LEN, D)
        dq_b = round_keep(d_query)
        dk_b = round_keep(d_key)
        dv_b = round_keep(d_value)
        d_input = d_resid1 + dense(dq_b, query_weight.T) + dense(dk_b, key_weight.T) + dense(dv_b, value_weight.T)
        terms = (dense(seq_rows.T, dq_b), dense(seq_rows.T, dk_b), dense(seq_rows.T, dv_b), lax.optimization_barrier(jnp.sum(d_query, axis=0)), lax.optimization_barrier(jnp.sum(d_value, axis=0)), output_grad, lax.optimization_barrier(jnp.sum(d_resid1, axis=0)), gain1_grad, shift1_grad, inner_grad, lax.optimization_barrier(jnp.sum(d_pre, axis=0)), outer_grad, lax.optimization_barrier(jnp.sum(d_resid2, axis=0)), gain2_grad, shift2_grad)
        totals = jax.tree.map(lambda left, right: left + right, totals, terms)
        return (totals, (block_out, d_input))
    zero_totals = (jnp.zeros((D, D), jnp.float32), jnp.zeros((D, D), jnp.float32), jnp.zeros((D, D), jnp.float32), jnp.zeros((D,), jnp.float32), jnp.zeros((D,), jnp.float32), jnp.zeros((D, D), jnp.float32), jnp.zeros((D,), jnp.float32), jnp.zeros((D,), jnp.float32), jnp.zeros((D,), jnp.float32), jnp.zeros((D, FF), jnp.float32), jnp.zeros((FF,), jnp.float32), jnp.zeros((FF, D), jnp.float32), jnp.zeros((D,), jnp.float32), jnp.zeros((D,), jnp.float32), jnp.zeros((D,), jnp.float32))
    inputs = (block_input.reshape(SEQUENCES, SEQ_LEN, D), cotangent.reshape(SEQUENCES, SEQ_LEN, D), lengths)
    totals, (outputs, input_grads) = lax.scan(one_sequence, zero_totals, inputs)
    return (outputs.reshape(TOKENS, D), input_grads.reshape(TOKENS, D)) + totals
```

```python
import functools
import types

import jax
import jax.numpy as jnp
from jax import lax
from jax.experimental import pallas as pl
from jax.experimental.pallas import tpu as pltpu
from jax.sharding import PartitionSpec as P

HEAD_DIM = 64
PAIR = 2 * HEAD_DIM
CHUNKS = 2
MESH = pl.DeviceIdType.MESH

inv_root2 = 0.7071067811865476
inv_root2pi = 0.3989422804014327
norm_eps = 1e-06
VMEM_LIMIT = 63 << 20


def dense(left, right):
    return jnp.dot(left, right, preferred_element_type=jnp.float32)


def dense_tn(left, right):
    return lax.dot_general(
        left, right, (((0,), (0,)), ((), ())), preferred_element_type=jnp.float32
    )


def dense_nt(left, right):
    return lax.dot_general(
        left, right, (((1,), (1,)), ((), ())), preferred_element_type=jnp.float32
    )


def mean_last(values):
    return jnp.mean(values, axis=-1, keepdims=True)


def norm_parts(resid):
    center = resid - mean_last(resid)
    inverse = lax.rsqrt(mean_last(center * center) + norm_eps)
    return center * inverse, inverse


def norm_back(normed, inverse, gain, upstream):
    scaled = upstream * gain
    return inverse * (scaled - mean_last(scaled) - normed * mean_last(scaled * normed))


def span(start, size):
    return pl.ds(pl.multiple_of(start, size), size)


class Place:
    def __init__(self):
        self.dp_size, self.tensor_size = lax.axis_size("dp"), lax.axis_size("tensor")
        self.quads, self.half = self.dp_size // 2, self.tensor_size // 2
        dp, tensor = lax.axis_index("dp"), lax.axis_index("tensor")
        self.q, self.c = lax.div(dp, 2), lax.rem(dp, 2)
        self.h, self.l = lax.div(tensor, self.half), lax.rem(tensor, self.half)
        self.rank = self.c * self.half + self.l
        self.column = self.c * self.tensor_size + tensor
        self.stays = self.c == self.h

    def at(self, q, c, h, l):
        return (2 * q + c, h * self.half + l)

    def beside(self):
        return self.at(self.q, 1 - self.c, self.h, self.l)

    def swapped(self):
        return self.at(self.q, self.h, self.c, self.l)

    def along(self, j):
        return lax.rem(self.l + j, self.half)

    def across(self, j):
        return lax.rem(self.q + j, self.quads)

    def column_peer(self, j):
        spot = lax.rem(self.column + j, 2 * self.tensor_size)
        c, tensor = lax.div(spot, self.tensor_size), lax.rem(spot, self.tensor_size)
        return spot, (2 * self.q + c, tensor)

    def greet(self):
        barrier = pltpu.get_barrier_semaphore()
        for j in range(1, 2 * self.tensor_size):
            pl.semaphore_signal(barrier, inc=1, device_id=self.column_peer(j)[1], device_id_type=MESH)
        for j in range(1, self.quads):
            other = self.at(self.across(j), self.c, self.h, self.l)
            pl.semaphore_signal(barrier, inc=1, device_id=other, device_id_type=MESH)
        pl.semaphore_wait(barrier, 2 * self.tensor_size + self.quads - 2)


class Mover:
    def __init__(self, place):
        self.place, self.open = place, []

    def send(self, source, target, send_sem, recv_sem, device, only=None):
        copy = pltpu.make_async_remote_copy(
            src_ref=source,
            dst_ref=target,
            send_sem=send_sem,
            recv_sem=recv_sem,
            device_id=device,
            device_id_type=MESH,
        )
        if only is None:
            copy.start()
        else:
            pl.when(only)(copy.start)
        self.open.append((copy, only))

    def keep_or_send(self, source, target, send_sem, recv_sem, device, is_self):
        self.send(source, target, send_sem, recv_sem, device, jnp.logical_not(is_self))
        pl.when(is_self)(pltpu.make_async_copy(source, target, recv_sem).start)

    def landed(self, target, recv_sem):
        pltpu.make_async_copy(target, target, recv_sem).wait()

    def since(self, mark):
        taken, self.open = self.open[mark:], self.open[:mark]
        return taken

    def finish(self, sends):
        for copy, only in sends:
            if only is None:
                copy.wait_send()
            else:
                pl.when(only)(copy.wait_send)

    def close(self):
        self.finish(self.since(0))


def rows_out(mv, buf, block_rows, chunk, send_sem, recv_sem):
    pc = mv.place
    size = block_rows // CHUNKS
    part = buf.at[span(pc.rank * block_rows + chunk * size, size)]
    for j in range(1, pc.half):
        other = pc.at(pc.q, pc.c, pc.h, pc.along(j))
        mv.send(part, part, send_sem.at[chunk, j], recv_sem.at[pc.rank, chunk], other)
    mv.send(part, part, send_sem.at[chunk, 0], recv_sem.at[pc.rank, chunk], pc.beside())


def rows_pass(mv, buf, block_rows, j, chunk, pass_sem, recv_sem):
    pc = mv.place
    size = block_rows // CHUNKS
    block = pc.c * pc.half + pc.along(j)
    part = buf.at[span(block * block_rows + chunk * size, size)]
    mv.landed(part, recv_sem.at[block, chunk])
    mv.send(part, part, pass_sem.at[chunk, j], recv_sem.at[block, chunk], pc.beside())


def rows_in(mv, buf, block_rows, j, chunk, recv_sem):
    pc = mv.place
    size = block_rows // CHUNKS
    block = (1 - pc.c) * pc.half + pc.along(j)
    part = buf.at[span(block * block_rows + chunk * size, size)]
    mv.landed(part, recv_sem.at[block, chunk])


def weights_out(mv, shard, dest, cols, seg, send_sem, recv_sem):
    pc = mv.place
    size = shard.shape[0]
    for half in range(2):
        mv.keep_or_send(
            shard.at[:, cols],
            dest.at[span((2 * pc.q + pc.c) * size, size), cols],
            send_sem.at[seg, half],
            recv_sem.at[seg, pc.c],
            pc.at(pc.q, pc.h, half, pc.l),
            jnp.logical_and(pc.stays, pc.h == half),
        )


def weights_pass(mv, size, dest, cols, seg, recv_sem, pass_sem, far_sem):
    pc = mv.place
    for c in range(2):
        mv.landed(dest.at[span((2 * pc.q + c) * size, size), cols], recv_sem.at[seg, c])
    both = dest.at[span(2 * pc.q * size, 2 * size), cols]
    for j in range(1, pc.quads):
        other = pc.at(pc.across(j), pc.c, pc.h, pc.l)
        mv.send(both, both, pass_sem.at[seg, j - 1], far_sem.at[seg, pc.quads - j - 1], other)


def weights_in(mv, size, dest, cols, seg, far_sem):
    pc = mv.place
    for j in range(1, pc.quads):
        part = dest.at[span(2 * pc.across(j) * size, 2 * size), cols]
        mv.landed(part, far_sem.at[seg, j - 1])


def gather_kernel(
    x_ref, w_ref, vec_ref, seq_ref, wide_ref, every_ref,
    swap_send, swap_recv, row_send, row_recv, row_pass_sem,
    w_send, w_recv, w_pass, w_far, v_send, v_recv, v_pass, v_far,
):
    pc = Place()
    mv = Mover(pc)
    own = x_ref.shape[0]
    size = own // CHUNKS
    shard = w_ref.shape[0]
    cols = pl.ds(0, w_ref.shape[1])
    pc.greet()
    spot = (2 * pc.q + pc.c) * pc.tensor_size + pc.h * pc.half + pc.l
    keep = pltpu.make_async_copy(vec_ref, every_ref.at[spot], v_recv.at[0])
    keep.start()
    for j in range(1, 2 * pc.tensor_size):
        mv.send(vec_ref, every_ref.at[spot], v_send.at[j], v_recv.at[2 * pc.tensor_size - j], pc.column_peer(j)[1])
    weights_out(mv, w_ref, wide_ref, cols, 0, w_send, w_recv)
    new_rank = pc.h * pc.half + pc.l
    for k in range(CHUNKS):
        mv.keep_or_send(
            x_ref.at[pl.ds(k * size, size)],
            seq_ref.at[span(new_rank * own + k * size, size)],
            swap_send.at[k],
            swap_recv.at[k],
            pc.swapped(),
            pc.stays,
        )
    keep.wait()
    for j in range(1, 2 * pc.tensor_size):
        mv.landed(every_ref.at[spot], v_recv.at[j])
    column = every_ref.at[span(2 * pc.q * pc.tensor_size, 2 * pc.tensor_size)]
    for j in range(1, pc.quads):
        other = pc.at(pc.across(j), pc.c, pc.h, pc.l)
        mv.send(column, column, v_pass.at[j - 1], v_far.at[pc.quads - j - 1], other)
    weights_pass(mv, shard, wide_ref, cols, 0, w_recv, w_pass, w_far)
    for k in range(CHUNKS):
        mv.landed(seq_ref.at[span(pc.rank * own + k * size, size)], swap_recv.at[k])
        rows_out(mv, seq_ref, own, k, row_send, row_recv)
    for j in range(1, pc.half):
        for k in range(CHUNKS):
            rows_pass(mv, seq_ref, own, j, k, row_pass_sem, row_recv)
    for j in range(pc.half):
        for k in range(CHUNKS):
            rows_in(mv, seq_ref, own, j, k, row_recv)
    for j in range(1, pc.quads):
        mv.landed(column, v_far.at[j - 1])
    weights_in(mv, shard, wide_ref, cols, 0, w_far)
    mv.close()


def gather_start(block_input, qkv_shard, vectors):
    dp_size, tensor_size = lax.axis_size("dp"), lax.axis_size("tensor")
    quads, half = dp_size // 2, tensor_size // 2
    dma = pltpu.SemaphoreType.DMA
    own, width = block_input.shape
    anywhere = pl.BlockSpec(memory_space=pl.ANY)
    return pl.pallas_call(
        gather_kernel,
        out_shape=[
            jax.ShapeDtypeStruct((own * tensor_size, width), jnp.bfloat16),
            jax.ShapeDtypeStruct((width, qkv_shard.shape[1]), jnp.bfloat16),
            jax.ShapeDtypeStruct((dp_size * tensor_size,) + vectors.shape, jnp.float32),
        ],
        in_specs=[anywhere] * 3,
        out_specs=[anywhere] * 3,
        scratch_shapes=[
            dma((CHUNKS,)), dma((CHUNKS,)),
            dma((CHUNKS, half)), dma((tensor_size, CHUNKS)), dma((CHUNKS, half)),
            dma((1, 2)), dma((1, 2)), dma((1, quads)), dma((1, quads)),
            dma((2 * tensor_size,)), dma((2 * tensor_size,)), dma((quads,)), dma((quads,)),
        ],
        compiler_params=pltpu.CompilerParams(
            collective_id=0, has_side_effects=True, vmem_limit_bytes=VMEM_LIMIT
        ),
        name="gather_start",
    )(block_input, qkv_shard, vectors)


def over_tiles(width, body):
    tile = min(256, width)

    def step(i, carry):
        body(span(i * tile, tile))
        return carry

    lax.fori_loop(0, width // tile, step, 0)


def reduce_rows(mv, s, sems, own, width, partial):
    pc = mv.place
    size = own // CHUNKS
    send_a, recv_a, send_z, recv_z = sems
    order = list(range(1, pc.half)) + [0]
    mark = len(mv.open)
    for j in order:
        block = (1 - pc.c) * pc.half + pc.along(j)

        def give(tile, j=j, block=block):
            s.core_out[j, :, tile] = partial(block, tile).astype(jnp.bfloat16)

        over_tiles(width, give)
        mv.send(s.core_out.at[j], s.core_in.at[j], send_a.at[j], recv_a.at[j], pc.beside())
    for j in order:
        block = pc.c * pc.half + pc.along(j)
        mv.landed(s.core_in.at[j], recv_a.at[j])
        if j:

            def add(tile, j=j, block=block):
                total = partial(block, tile) + s.core_in[j, :, tile].astype(jnp.float32)
                s.chip_out[j - 1, :, tile] = total.astype(jnp.bfloat16)

            over_tiles(width, add)
            other = pc.at(pc.q, pc.c, pc.h, pc.along(j))
            for k in range(CHUNKS):
                rows = pl.ds(k * size, size)
                mv.send(
                    s.chip_out.at[j - 1, rows],
                    s.chip_in.at[pc.half - j - 1, rows],
                    send_z.at[j, k],
                    recv_z.at[pc.half - j, k],
                    other,
                )
        else:

            def hold(tile, block=block):
                total = partial(block, tile) + s.core_in[0, :, tile].astype(jnp.float32)
                s.held[:, tile] = total

            over_tiles(width, hold)
    return mv.since(mark)


def reduced_chunk(mv, s, sems, own, k):
    pc = mv.place
    size = own // CHUNKS
    rows = pl.ds(k * size, size)
    total = s.held[rows, :]
    for j in range(1, pc.half):
        mv.landed(s.chip_in.at[j - 1, rows], sems[3].at[j, k])
        total = total + s.chip_in[j - 1, rows, :].astype(jnp.float32)
    return total


def in_order(mv, buf, own, pass_sem, recv_sem, work):
    pc = mv.place
    for j in range(pc.half):
        if j:
            for k in range(CHUNKS):
                rows_pass(mv, buf, own, j, k, pass_sem, recv_sem)
        work(pc.c * pc.half + pc.along(j))
        for k in range(CHUNKS):
            rows_in(mv, buf, own, j, k, recv_sem)
        work((1 - pc.c) * pc.half + pc.along(j))


def to_group(mv, own, source, target, send_sem, recv_sem):
    pc = mv.place
    size = pc.tensor_size
    for j in range(1, size):
        rank = lax.rem(pc.rank + j, size)
        other = pc.at(pc.q, lax.div(rank, pc.half), pc.h, lax.rem(rank, pc.half))
        mv.send(source(rank), target, send_sem.at[j], recv_sem.at[size - j], other)


def grad_out(mv, s, shard, start, width, left, right, seg):
    pc = mv.place
    cols = pl.ds(start, width)

    def fill_rows(rows):
        def fill(tile):
            tile_at = pl.ds(pl.multiple_of(start + tile.start, tile.size), tile.size)
            s.grads[rows, tile_at] = dense_tn(left(rows), right(tile)).astype(jnp.bfloat16)

        over_tiles(width, fill)

    by_quad = 2 * shard % 128 == 0
    if not by_quad:
        for at in range(0, s.grads.shape[0], 128):
            fill_rows(pl.ds(at, 128))
    for j in list(range(1, pc.quads)) + [0]:
        quad = pc.across(j)
        rows = span(2 * shard * quad, 2 * shard)
        if by_quad:
            fill_rows(rows)
        if j:
            mv.send(
                s.grads.at[rows, cols],
                s.grads_in.at[pc.quads - j - 1, :, cols],
                s.grad_send.at[seg, j],
                s.grad_recv.at[seg, pc.quads - j],
                pc.at(quad, pc.c, pc.h, pc.l),
            )


def grad_sum(mv, s, shard, start, width, seg, result):
    pc = mv.place
    cols = pl.ds(start, width)
    for j in range(1, pc.quads):
        mv.landed(s.grads_in.at[j - 1, :, cols], s.grad_recv.at[seg, j])

    def total(tile):
        tile_at = pl.ds(pl.multiple_of(start + tile.start, tile.size), tile.size)
        value = s.grads[span(2 * shard * pc.q, 2 * shard), tile_at].astype(jnp.float32)
        for j in range(1, pc.quads):
            value = value + s.grads_in[j - 1, :, tile_at].astype(jnp.float32)
        s.grads_out[:, tile_at] = value.astype(jnp.bfloat16)

    over_tiles(width, total)
    for core in range(2):
        mv.keep_or_send(
            s.grads_out.at[pl.ds(core * shard, shard), cols],
            result.at[pc.h, :, cols],
            s.owner_send.at[seg, core],
            s.owner_recv.at[seg, pc.h],
            pc.at(pc.q, core, pc.c, pc.l),
            jnp.logical_and(pc.stays, pc.c == core),
        )


def layer_kernel(names, *refs):
    by_name = dict(zip(names, refs))
    s = types.SimpleNamespace(**by_name)
    sems_ra = (s.ra_send_a, s.ra_recv_a, s.ra_send_z, s.ra_recv_z)
    sems_rb = (s.rb_send_a, s.rb_recv_a, s.rb_send_z, s.rb_recv_z)
    sems_rc = (s.rc_send_a, s.rc_recv_a, s.rc_send_z, s.rc_recv_z)
    pc = Place()
    mv = Mover(pc)
    seq, wide, rest, cot = s.seq, s.wide, s.rest, s.cot
    own = cot.shape[0]
    size = own // CHUNKS
    total_rows, width = seq.shape
    heads = wide.shape[1] // 3
    hidden = s.inner.shape[1] // 2
    shard = rest.shape[0]
    group = pc.tensor_size
    pairs = heads // PAIR
    mine = span(pc.rank * own, own)
    vec, sums = s.vec, s.sums
    f32 = jnp.float32
    inner, hid_cols, out_cols = s.inner, pl.ds(0, hidden), pl.ds(hidden, hidden)
    scale = HEAD_DIM ** (-0.5)

    def block_rows(block):
        return span(block * own, own)

    def own_chunk(k):
        return span(pc.rank * own + k * size, size)

    pc.greet()

    def weight_parts():
        base_new = (pc.h * pc.half + pc.l) * width
        base = pc.rank * width
        new_out = s.out_all.at[span(base_new, width)]
        my_out = s.out_all.at[span(base, width)]
        return (
            (rest.at[:, pl.ds(0, heads)], new_out, my_out, pl.ds(0, heads)),
            (rest.at[:, pl.ds(heads, hidden)], inner, inner, hid_cols),
            (rest.at[:, pl.ds(heads + hidden, hidden)], inner, inner, out_cols),
        )

    parts = weight_parts()

    def start_weight(seg):
        source, target, _, cols = parts[seg]
        place = span((2 * pc.q + pc.c) * shard, shard)
        for half in range(2):
            mv.keep_or_send(
                source,
                target.at[place, cols],
                s.w_send.at[seg, half],
                s.w_recv.at[seg, pc.c],
                pc.at(pc.q, pc.h, half, pc.l),
                jnp.logical_and(pc.stays, pc.h == half),
            )

    def pass_weight(seg):
        weights_pass(mv, shard, parts[seg][2], parts[seg][3], seg, s.w_recv, s.w_pass, s.w_far)

    def end_weight(seg):
        weights_in(mv, shard, parts[seg][2], parts[seg][3], seg, s.w_far)

    for seg in range(3):
        start_weight(seg)
    mv.keep_or_send(cot, s.cot_in, s.cot_send.at[0], s.cot_recv.at[0], pc.swapped(), pc.stays)
    sums[...] = jnp.zeros_like(sums)

    big = min(512, total_rows)
    qkv = s.qkv

    def project(i, carry):
        rows = span(i * big, big)
        query = (dense(seq[rows, :], wide[:, 0:heads]) + vec[6:7, 0:heads]).astype(jnp.bfloat16)
        qkv[rows, 0:heads] = (query.astype(f32) * scale).astype(jnp.bfloat16)
        qkv[rows, heads : 2 * heads] = dense(seq[rows, :], wide[:, heads : 2 * heads]).astype(jnp.bfloat16)
        value = dense(seq[rows, :], wide[:, 2 * heads : 3 * heads]) + vec[6:7, heads : 2 * heads]
        qkv[rows, 2 * heads : 3 * heads] = value.astype(jnp.bfloat16)
        return carry

    lax.fori_loop(0, total_rows // big, project, 0)
    pass_weight(0)

    step_rows = min(256, total_rows)
    spot = lax.broadcasted_iota(jnp.int32, (1, total_rows), 1).astype(f32)
    bias = jnp.where(spot < s.length[0:1, 0:1], 0.0, -jnp.inf).astype(f32)

    def head_cols(pair, head, part):
        start = part * heads + pair * PAIR + head * HEAD_DIM
        return slice(start, start + HEAD_DIM)

    for pair in range(pairs):

        def attend(i, carry, pair=pair):
            rows = span(i * step_rows, step_rows)
            found = []
            for head in range(2):
                scores = dense_nt(qkv[rows, head_cols(pair, head, 0)], qkv[:, head_cols(pair, head, 1)]) + bias
                top = jnp.max(scores, axis=-1, keepdims=True)
                grown = jnp.exp(scores - top)
                total = jnp.sum(grown, axis=-1, keepdims=True)
                probs = (grown * (1.0 / total)).astype(jnp.bfloat16)
                lane = 2 * pair + head
                s.log_total[rows, lane : lane + 1] = top + jnp.log(total)
                found.append(dense(probs, qkv[:, head_cols(pair, head, 2)]))
            s.ctx[rows, pair * PAIR : (pair + 1) * PAIR] = jnp.concatenate(found, axis=1).astype(jnp.bfloat16)
            return carry

        lax.fori_loop(0, total_rows // step_rows, attend, 0)
        place = span(pc.rank * heads + pair * PAIR, PAIR)
        pair_cols = pl.ds(pair * PAIR, PAIR)
        to_group(
            mv, own,
            lambda rank, cols=pair_cols: s.ctx.at[span(rank * own, own), cols],
            s.own_ctx.at[:, place],
            s.ctx_send.at[pair], s.ctx_recv.at[pair],
        )
        s.own_ctx[:, place] = s.ctx[mine, pair_cols]
        if pair == 0:
            end_weight(0)
            for k in range(CHUNKS):
                rows_out(mv, s.out_all, width, k, s.out_send, s.out_recv)
            pass_weight(1)
    for j in range(1, pc.half):
        for k in range(CHUNKS):
            rows_pass(mv, s.out_all, width, j, k, s.out_pass, s.out_recv)
    for pair in range(pairs):
        for j in range(1, group):
            mv.landed(s.own_ctx.at[:, pl.ds(0, PAIR)], s.ctx_recv.at[pair, j])
    for j in range(pc.half):
        for k in range(CHUNKS):
            rows_in(mv, s.out_all, width, j, k, s.out_recv)

    for k in range(CHUNKS):
        rows = pl.ds(k * size, size)
        total = seq[own_chunk(k), :].astype(f32) + vec[0:1, :]
        for t in range(group):
            total = total + dense_nt(
                s.own_ctx[rows, t * heads : (t + 1) * heads], s.out_all[t * width : (t + 1) * width, :]
            )
        s.resid[rows, :] = total
        normed, _ = norm_parts(total)
        middle = normed * vec[1:2, :] + vec[2:3, :]
        s.middle[rows, :] = middle
        s.mid_rows[own_chunk(k), :] = middle.astype(jnp.bfloat16)
        rows_out(mv, s.mid_rows, own, k, s.mid_send, s.mid_recv)
    pass_weight(2)

    end_weight(1)

    def expand(block):
        rows = block_rows(block)

        def one(tile):
            pre = dense(s.mid_rows[rows, :], inner[:, tile]) + vec[7:8, tile]
            cdf = 0.5 * (1.0 + lax.erf(pre * inv_root2))
            s.hid[rows, tile] = (pre * cdf).astype(jnp.bfloat16)
            s.slope[rows, tile] = cdf + pre * inv_root2pi * jnp.exp(-0.5 * pre * pre)

        over_tiles(hidden, one)

    in_order(mv, s.mid_rows, own, s.mid_pass, s.mid_recv, expand)
    end_weight(2)
    sent_ra = reduce_rows(
        mv, s, sems_ra, own, width,
        lambda block, tile: dense_nt(s.hid[block_rows(block), :], inner[tile, out_cols]),
    )
    mv.landed(s.cot_in, s.cot_recv.at[0])
    for k in range(CHUNKS):
        rows = pl.ds(k * size, size)
        total = s.middle[rows, :] + reduced_chunk(mv, s, sems_ra, own, k) + vec[3:4, :]
        normed, inverse = norm_parts(total)
        up = s.cot_in[rows, :].astype(f32)
        d_resid = norm_back(normed, inverse, vec[4:5, :], up)
        s.d_resid[rows, :] = d_resid
        s.ffn_rows[own_chunk(k), :] = d_resid.astype(jnp.bfloat16)
        rows_out(mv, s.ffn_rows, own, k, s.ffn_send, s.ffn_recv)
        sums[3:4, :] += jnp.sum(d_resid, axis=0, keepdims=True)
        sums[4:5, :] += jnp.sum(up * normed, axis=0, keepdims=True)
        sums[5:6, :] += jnp.sum(up, axis=0, keepdims=True)
        s.out_stage[rows, :] = (normed * vec[4:5, :] + vec[5:6, :]).astype(jnp.bfloat16)
        mv.keep_or_send(
            s.out_stage.at[rows], s.block_out.at[rows],
            s.bo_send.at[k], s.bo_recv.at[k], pc.swapped(), pc.stays,
        )

    mv.finish(sent_ra)

    def shrink(block):
        rows = block_rows(block)

        def one(tile):
            shifted = pl.ds(pl.multiple_of(hidden + tile.start, tile.size), tile.size)
            d_pre = dense(s.ffn_rows[rows, :], inner[:, shifted]) * s.slope[rows, tile]
            sums[7:8, tile] += jnp.sum(d_pre, axis=0, keepdims=True)
            s.d_pre[rows, tile] = d_pre.astype(jnp.bfloat16)

        over_tiles(hidden, one)

    in_order(mv, s.ffn_rows, own, s.ffn_pass, s.ffn_recv, shrink)
    sent_rb = reduce_rows(
        mv, s, sems_rb, own, width,
        lambda block, tile: dense_nt(s.d_pre[block_rows(block), :], inner[tile, hid_cols]),
    )
    at_out, at_in, at_outer = 3 * heads, 4 * heads, 4 * heads + hidden
    grad_out(
        mv, s, shard, at_outer, hidden,
        lambda rows: s.ffn_rows[:, rows], lambda tile: s.hid[:, tile], 0,
    )
    grad_out(
        mv, s, shard, at_in, hidden,
        lambda rows: s.mid_rows[:, rows], lambda tile: s.d_pre[:, tile], 1,
    )
    for k in range(CHUNKS):
        rows = pl.ds(k * size, size)
        up = reduced_chunk(mv, s, sems_rb, own, k) + s.d_resid[rows, :]
        normed, inverse = norm_parts(s.resid[rows, :])
        d_resid = norm_back(normed, inverse, vec[1:2, :], up)
        s.d_resid[rows, :] = d_resid
        s.attn_rows[own_chunk(k), :] = d_resid.astype(jnp.bfloat16)
        sums[0:1, :] += jnp.sum(d_resid, axis=0, keepdims=True)
        sums[1:2, :] += jnp.sum(up * normed, axis=0, keepdims=True)
        sums[2:3, :] += jnp.sum(up, axis=0, keepdims=True)

    mv.finish(sent_rb)

    for t in range(group):
        s.d_ctx_out[t, :, :] = dense(
            s.attn_rows[mine, :], s.out_all[t * width : (t + 1) * width, :]
        ).astype(jnp.bfloat16)
    to_group(
        mv, own,
        lambda rank: s.d_ctx_out.at[rank],
        s.d_ctx.at[mine],
        s.d_ctx_send, s.d_ctx_recv,
    )
    s.d_ctx[mine, :] = s.d_ctx_out[pc.rank, :, :]
    for k in range(CHUNKS):
        rows_out(mv, s.attn_rows, own, k, s.at_send, s.at_recv)
    for j in range(1, group):
        mv.landed(s.d_ctx.at[mine], s.d_ctx_recv.at[j])
    d_qkv = s.d_qkv
    for pair in range(pairs):
        s.key_sum[...] = jnp.zeros_like(s.key_sum)
        s.value_sum[...] = jnp.zeros_like(s.value_sum)

        def attend_back(i, carry, pair=pair):
            rows = span(i * step_rows, step_rows)
            found = []
            for head in range(2):
                cols = slice(head * HEAD_DIM, (head + 1) * HEAD_DIM)
                lane = 2 * pair + head
                query, key = qkv[rows, head_cols(pair, head, 0)], qkv[:, head_cols(pair, head, 1)]
                grad = s.d_ctx[rows, head_cols(pair, head, 0)]
                scores = dense_nt(query, key) + bias
                probs = jnp.exp(scores - s.log_total[rows, lane : lane + 1])
                d_probs = dense_nt(grad, qkv[:, head_cols(pair, head, 2)])
                within = jnp.sum(probs * d_probs, axis=-1, keepdims=True)
                d_scores = (probs * (d_probs - within)).astype(jnp.bfloat16)
                found.append(dense(d_scores, key) * scale)
                s.value_sum[cols, :] += dense_tn(grad, probs.astype(jnp.bfloat16))
                s.key_sum[cols, :] += dense_tn(query, d_scores)
            d_query = jnp.concatenate(found, axis=1)
            d_qkv[rows, pair * PAIR : (pair + 1) * PAIR] = d_query.astype(jnp.bfloat16)
            sums[6:7, pair * PAIR : (pair + 1) * PAIR] += jnp.sum(d_query, axis=0, keepdims=True)
            return carry

        lax.fori_loop(0, total_rows // step_rows, attend_back, 0)
        at_key = slice(heads + pair * PAIR, heads + (pair + 1) * PAIR)
        at_value = slice(2 * heads + pair * PAIR, 2 * heads + (pair + 1) * PAIR)
        d_qkv[:, at_key] = jnp.transpose(s.key_sum[...]).astype(jnp.bfloat16)
        d_value = jnp.transpose(s.value_sum[...])
        d_qkv[:, at_value] = d_value.astype(jnp.bfloat16)
        sums[6:7, at_key] = jnp.sum(d_value, axis=0, keepdims=True)
        if pair == 0:
            for j in range(1, pc.half):
                for k in range(CHUNKS):
                    rows_pass(mv, s.attn_rows, own, j, k, s.at_pass, s.at_recv)
            for j in range(pc.half):
                for k in range(CHUNKS):
                    rows_in(mv, s.attn_rows, own, j, k, s.at_recv)
            grad_out(
                mv, s, shard, at_out, heads,
                lambda rows: s.attn_rows[:, rows], lambda tile: s.ctx[:, tile], 2,
            )
    slots = s.sum_slots
    slots[pc.column] = sums[...]
    for j in range(1, 2 * group):
        mv.send(
            sums, slots.at[pc.column],
            s.sum_send.at[j], s.sum_recv.at[2 * group - j], pc.column_peer(j)[1],
        )
    sent_rc = reduce_rows(
        mv, s, sems_rc, own, width,
        lambda block, tile: dense_nt(d_qkv[block_rows(block), :], wide[tile, :]),
    )
    grad_out(
        mv, s, shard, 0, 3 * heads,
        lambda rows: seq[:, rows], lambda tile: d_qkv[:, tile], 3,
    )
    for k in range(CHUNKS):
        rows = pl.ds(k * size, size)
        s.ig_stage[rows, :] = (reduced_chunk(mv, s, sems_rc, own, k) + s.d_resid[rows, :]).astype(jnp.bfloat16)
        mv.keep_or_send(
            s.ig_stage.at[rows], s.input_grad.at[rows],
            s.ig_send.at[k], s.ig_recv.at[k], pc.swapped(), pc.stays,
        )
    mv.finish(sent_rc)
    for j in range(1, 2 * group):
        mv.landed(slots.at[0], s.sum_recv.at[j])
    every = slots[0]
    for j in range(1, 2 * group):
        every = every + slots[j]
    chosen = pc.h * group + pc.l
    biases = slots[chosen] + slots[chosen + pc.half]
    row = lax.broadcasted_iota(jnp.int32, every.shape, 0)
    summed = jnp.where(row < 6, every, biases)
    s.sum_stage[...] = summed
    for j in range(1, pc.quads):
        other = pc.at(pc.across(j), pc.c, pc.h, pc.l)
        mv.send(s.sum_stage, s.sum_far.at[pc.quads - j - 1], s.far_send.at[j], s.far_recv.at[pc.quads - j], other)
    grad_sum(mv, s, shard, at_outer, hidden, 0, s.weight_grads)
    grad_sum(mv, s, shard, at_in, hidden, 1, s.weight_grads)
    grad_sum(mv, s, shard, at_out, heads, 2, s.weight_grads)
    for j in range(1, pc.quads):
        mv.landed(s.sum_stage, s.far_recv.at[j])
        summed = summed + s.sum_far[j - 1]
    s.vec_grads[...] = summed
    grad_sum(mv, s, shard, 0, 3 * heads, 3, s.weight_grads)
    for k in range(CHUNKS):
        rows = pl.ds(k * size, size)
        mv.landed(s.block_out.at[rows], s.bo_recv.at[k])
        mv.landed(s.input_grad.at[rows], s.ig_recv.at[k])
    for seg, (start, count) in enumerate(
        ((at_outer, hidden), (at_in, hidden), (at_out, heads), (0, 3 * heads))
    ):
        for h in range(2):
            mv.landed(s.weight_grads.at[h, :, pl.ds(start, count)], s.owner_recv.at[seg, h])
    mv.close()


def run_layer(seq, wide, rest, cot, vec, length):
    dp_size, tensor_size = lax.axis_size("dp"), lax.axis_size("tensor")
    quads, half = dp_size // 2, tensor_size // 2
    rows, width = seq.shape
    own = rows // tensor_size
    heads = wide.shape[1] // 3
    shard = rest.shape[0]
    hidden = (rest.shape[1] - heads) // 2
    pairs = heads // PAIR
    every = 4 * heads + 2 * hidden
    bf16, f32 = jnp.bfloat16, jnp.float32
    ins = dict(seq=seq, wide=wide, rest=rest, cot=cot, vec=vec, length=length)
    outs = dict(
        block_out=((own, width), bf16),
        input_grad=((own, width), bf16),
        weight_grads=((2, shard, every), bf16),
        vec_grads=((8, width), f32),
    )
    buffers = dict(
        inner=((width, 2 * hidden), bf16),
        out_all=((tensor_size * width, heads), bf16),
        qkv=((rows, 3 * heads), bf16),
        log_total=((rows, 128), f32),
        ctx=((rows, heads), bf16),
        own_ctx=((own, width), bf16),
        resid=((own, width), f32),
        middle=((own, width), f32),
        d_resid=((own, width), f32),
        held=((own, width), f32),
        mid_rows=((rows, width), bf16),
        slope=((rows, hidden), f32),
        hid=((rows, hidden), bf16),
        ffn_rows=((rows, width), bf16),
        d_pre=((rows, hidden), bf16),
        attn_rows=((rows, width), bf16),
        d_ctx_out=((tensor_size, own, heads), bf16),
        d_ctx=((rows, heads), bf16),
        d_qkv=((rows, 3 * heads), bf16),
        key_sum=((PAIR, rows), f32),
        value_sum=((PAIR, rows), f32),
        core_out=((half, own, width), bf16),
        core_in=((half, own, width), bf16),
        chip_out=((half - 1, own, width), bf16),
        chip_in=((half - 1, own, width), bf16),
        grads=((width, every), bf16),
        grads_in=((quads - 1, 2 * shard, every), bf16),
        grads_out=((2 * shard, every), bf16),
        cot_in=((own, width), bf16),
        out_stage=((own, width), bf16),
        ig_stage=((own, width), bf16),
        sums=((8, width), f32),
        sum_slots=((2 * tensor_size, 8, width), f32),
        sum_stage=((8, width), f32),
        sum_far=((quads - 1, 8, width), f32),
    )
    sems = dict(
        w_send=(3, 2), w_recv=(3, 2), w_pass=(3, quads), w_far=(3, quads),
        cot_send=(1,), cot_recv=(1,),
        ctx_send=(pairs, tensor_size), ctx_recv=(pairs, tensor_size),
        d_ctx_send=(tensor_size,), d_ctx_recv=(tensor_size,),
        bo_send=(CHUNKS,), bo_recv=(CHUNKS,), ig_send=(CHUNKS,), ig_recv=(CHUNKS,),
        grad_send=(4, quads), grad_recv=(4, quads), owner_send=(4, 2), owner_recv=(4, 2),
        sum_send=(2 * tensor_size,), sum_recv=(2 * tensor_size,), far_send=(quads,), far_recv=(quads,),
    )
    for tag in ("out", "mid", "ffn", "at"):
        sems[tag + "_send"] = (CHUNKS, half)
        sems[tag + "_recv"] = (tensor_size, CHUNKS)
        sems[tag + "_pass"] = (CHUNKS, half)
    for tag in ("ra", "rb", "rc"):
        sems[tag + "_send_a"] = (half,)
        sems[tag + "_recv_a"] = (half,)
        sems[tag + "_send_z"] = (half, CHUNKS)
        sems[tag + "_recv_z"] = (half, CHUNKS)
    names = tuple(ins) + tuple(outs) + tuple(buffers) + tuple(sems)
    vmem = pl.BlockSpec(memory_space=pltpu.VMEM)
    return pl.pallas_call(
        functools.partial(layer_kernel, names),
        out_shape=[jax.ShapeDtypeStruct(shape, kind) for shape, kind in outs.values()],
        in_specs=[vmem] * len(ins),
        out_specs=[vmem] * len(outs),
        scratch_shapes=[pltpu.VMEM(shape, kind) for shape, kind in buffers.values()]
        + [pltpu.SemaphoreType.DMA(shape) for shape in sems.values()],
        compiler_params=pltpu.CompilerParams(
            collective_id=1, has_side_effects=True, vmem_limit_bytes=VMEM_LIMIT
        ),
        name="layer",
    )(*ins.values())


def per_device(
    block_input,
    lengths,
    query_weight,
    key_weight,
    value_weight,
    query_bias,
    value_bias,
    output_weight,
    output_bias,
    first_gain,
    first_shift,
    inner_weight,
    inner_bias,
    outer_weight,
    outer_bias,
    second_gain,
    second_shift,
    cotangent,
):
    f32 = jnp.float32
    dp_size, tensor_size = lax.axis_size("dp"), lax.axis_size("tensor")
    half = tensor_size // 2
    dp, tensor = lax.axis_index("dp"), lax.axis_index("tensor")
    c, h, l = dp % 2, tensor // half, tensor % half
    rank, sequence = c * half + l, dp - c + h

    features = (output_bias, first_gain, first_shift, outer_bias, second_gain, second_shift)
    biases = (query_bias, value_bias, inner_bias)
    packed = jnp.concatenate(
        list(features) + [bias.astype(f32) for bias in biases] + [lengths.astype(f32)]
    )
    lines = -(-packed.shape[0] // 1024) * 8
    packed = jnp.pad(packed, (0, lines * 128 - packed.shape[0])).reshape(lines, 128)
    qkv_shard = jnp.concatenate([query_weight, key_weight, value_weight], axis=1)
    rest = jnp.concatenate([output_weight.T, inner_weight, outer_weight.T], axis=1)
    seq, wide, every = gather_start(block_input, qkv_shard, packed)

    width = block_input.shape[1]
    every = every.reshape(dp_size, tensor_size, -1)
    full, start = [], 0
    for part in features:
        full.append(every[:, :, start : start + part.shape[0]].reshape(1, width))
        start += part.shape[0]
    own = lax.dynamic_index_in_dim(every, rank, 1, keepdims=False)
    bias_full = []
    for part in biases:
        bias_full.append(own[:, start : start + part.shape[0]].reshape(1, -1))
        start += part.shape[0]
    length = lax.dynamic_index_in_dim(every[:, 0, start : start + 1], sequence, 0)
    length = jnp.broadcast_to(length, (8, 128))

    def pad(row):
        return jnp.pad(row, ((0, 0), (0, width - row.shape[1])))

    vec = jnp.concatenate(
        full + [pad(jnp.concatenate(bias_full[:2], axis=1)), pad(bias_full[2])], axis=0
    )
    block_out, input_grad, weight_grads, vec_grads = run_layer(seq, wide, rest, cotangent, vec, length)

    heads, hidden = query_weight.shape[1], inner_weight.shape[1]
    both = weight_grads[0].astype(f32) + weight_grads[1].astype(f32)
    cuts = [0, heads, 2 * heads, 3 * heads, 4 * heads, 4 * heads + hidden, 4 * heads + 2 * hidden]
    pieces = [both[:, a:b] for a, b in zip(cuts[:-1], cuts[1:])]
    piece = width // (dp_size * tensor_size)
    mine = lax.dynamic_slice_in_dim(vec_grads, (dp * tensor_size + tensor) * piece, piece, axis=1)

    def bias_piece(row, start, count):
        size = count // dp_size
        return lax.dynamic_slice(vec_grads, (row, start + dp * size), (1, size))[0]

    return (
        block_out,
        input_grad.astype(f32),
        pieces[0],
        pieces[1],
        pieces[2],
        bias_piece(6, 0, heads),
        bias_piece(6, heads, heads),
        pieces[3].T,
        mine[0],
        mine[1],
        mine[2],
        pieces[4],
        bias_piece(7, 0, hidden),
        pieces[5].T,
        mine[3],
        mine[4],
        mine[5],
    )


def solution(mesh):
    return jax.shard_map(
        per_device,
        mesh=mesh,
        in_specs=(
            P(("dp", "tensor"), None),
            P("dp"),
            P("dp", "tensor"),
            P("dp", "tensor"),
            P("dp", "tensor"),
            P(("tensor", "dp")),
            P(("tensor", "dp")),
            P("tensor", "dp"),
            P(("dp", "tensor")),
            P(("dp", "tensor")),
            P(("dp", "tensor")),
            P("dp", "tensor"),
            P(("tensor", "dp")),
            P("tensor", "dp"),
            P(("dp", "tensor")),
            P(("dp", "tensor")),
            P(("dp", "tensor")),
            P(("dp", "tensor"), None),
        ),
        out_specs=(
            P(("dp", "tensor"), None),
            P(("dp", "tensor"), None),
            P("dp", "tensor"),
            P("dp", "tensor"),
            P("dp", "tensor"),
            P(("tensor", "dp")),
            P(("tensor", "dp")),
            P("tensor", "dp"),
            P(("dp", "tensor")),
            P(("dp", "tensor")),
            P(("dp", "tensor")),
            P("dp", "tensor"),
            P(("tensor", "dp")),
            P("tensor", "dp"),
            P(("dp", "tensor")),
            P(("dp", "tensor")),
            P(("dp", "tensor")),
        ),
        check_vma=False,
    )
```

```python
import functools
import types

import jax
import jax.numpy as jnp
from jax import lax
from jax.experimental import pallas as pl
from jax.experimental.pallas import tpu as pltpu
from jax.sharding import PartitionSpec as P

HEAD_DIM = 64
PAIR = 2 * HEAD_DIM
CHUNKS = 2
MESH = pl.DeviceIdType.MESH

inv_root2 = 0.7071067811865476
inv_root2pi = 0.3989422804014327
norm_eps = 1e-06
VMEM_LIMIT = 63 << 20


def dense(left, right):
    return jnp.dot(left, right, preferred_element_type=jnp.float32)


def dense_tn(left, right):
    return lax.dot_general(
        left, right, (((0,), (0,)), ((), ())), preferred_element_type=jnp.float32
    )


def dense_nt(left, right):
    return lax.dot_general(
        left, right, (((1,), (1,)), ((), ())), preferred_element_type=jnp.float32
    )


def mean_last(values):
    return jnp.mean(values, axis=-1, keepdims=True)


def norm_parts(resid):
    center = resid - mean_last(resid)
    inverse = lax.rsqrt(mean_last(center * center) + norm_eps)
    return center * inverse, inverse


def norm_back(normed, inverse, gain, upstream):
    scaled = upstream * gain
    return inverse * (scaled - mean_last(scaled) - normed * mean_last(scaled * normed))


def span(start, size):
    return pl.ds(pl.multiple_of(start, size), size)


class Place:
    def __init__(self):
        self.dp_size, self.tensor_size = lax.axis_size("dp"), lax.axis_size("tensor")
        self.quads, self.half = self.dp_size // 2, self.tensor_size // 2
        dp, tensor = lax.axis_index("dp"), lax.axis_index("tensor")
        self.q, self.c = lax.div(dp, 2), lax.rem(dp, 2)
        self.h, self.l = lax.div(tensor, self.half), lax.rem(tensor, self.half)
        self.rank = self.c * self.half + self.l
        self.column = self.c * self.tensor_size + tensor
        self.stays = self.c == self.h

    def at(self, q, c, h, l):
        return (2 * q + c, h * self.half + l)

    def beside(self):
        return self.at(self.q, 1 - self.c, self.h, self.l)

    def swapped(self):
        return self.at(self.q, self.h, self.c, self.l)

    def along(self, j):
        return lax.rem(self.l + j, self.half)

    def across(self, j):
        return lax.rem(self.q + j, self.quads)

    def quad_pair(self):
        x, y = lax.rem(self.q, 2), lax.div(self.q, 2)
        return 2 * y + 1 - x, 2 * (1 - y) + x, 2 * (1 - y) + 1 - x

    def in_quad(self, q):
        return self.at(q, self.c, self.h, self.l)

    def column_peer(self, j):
        spot = lax.rem(self.column + j, 2 * self.tensor_size)
        c, tensor = lax.div(spot, self.tensor_size), lax.rem(spot, self.tensor_size)
        return spot, (2 * self.q + c, tensor)

    def greet(self):
        barrier = pltpu.get_barrier_semaphore()
        for j in range(1, 2 * self.tensor_size):
            pl.semaphore_signal(barrier, inc=1, device_id=self.column_peer(j)[1], device_id_type=MESH)
        for j in range(1, self.quads):
            other = self.at(self.across(j), self.c, self.h, self.l)
            pl.semaphore_signal(barrier, inc=1, device_id=other, device_id_type=MESH)
        pl.semaphore_wait(barrier, 2 * self.tensor_size + self.quads - 2)


class Mover:
    def __init__(self, place):
        self.place, self.open = place, []

    def send(self, source, target, send_sem, recv_sem, device, only=None):
        copy = pltpu.make_async_remote_copy(
            src_ref=source,
            dst_ref=target,
            send_sem=send_sem,
            recv_sem=recv_sem,
            device_id=device,
            device_id_type=MESH,
        )
        if only is None:
            copy.start()
        else:
            pl.when(only)(copy.start)
        self.open.append((copy, only))

    def keep_or_send(self, source, target, send_sem, recv_sem, device, is_self):
        self.send(source, target, send_sem, recv_sem, device, jnp.logical_not(is_self))
        pl.when(is_self)(pltpu.make_async_copy(source, target, recv_sem).start)

    def landed(self, target, recv_sem):
        pltpu.make_async_copy(target, target, recv_sem).wait()

    def since(self, mark):
        taken, self.open = self.open[mark:], self.open[:mark]
        return taken

    def finish(self, sends):
        for copy, only in sends:
            if only is None:
                copy.wait_send()
            else:
                pl.when(only)(copy.wait_send)

    def close(self):
        self.finish(self.since(0))


def rows_out(mv, buf, block_rows, chunk, send_sem, recv_sem):
    pc = mv.place
    size = block_rows // CHUNKS
    part = buf.at[span(pc.rank * block_rows + chunk * size, size)]
    for j in range(1, pc.half):
        other = pc.at(pc.q, pc.c, pc.h, pc.along(j))
        mv.send(part, part, send_sem.at[chunk, j], recv_sem.at[pc.rank, chunk], other)
    mv.send(part, part, send_sem.at[chunk, 0], recv_sem.at[pc.rank, chunk], pc.beside())


def rows_pass(mv, buf, block_rows, j, chunk, pass_sem, recv_sem):
    pc = mv.place
    size = block_rows // CHUNKS
    block = pc.c * pc.half + pc.along(j)
    part = buf.at[span(block * block_rows + chunk * size, size)]
    mv.landed(part, recv_sem.at[block, chunk])
    mv.send(part, part, pass_sem.at[chunk, j], recv_sem.at[block, chunk], pc.beside())


def rows_in(mv, buf, block_rows, j, chunk, recv_sem):
    pc = mv.place
    size = block_rows // CHUNKS
    block = (1 - pc.c) * pc.half + pc.along(j)
    part = buf.at[span(block * block_rows + chunk * size, size)]
    mv.landed(part, recv_sem.at[block, chunk])


def weights_pass(mv, size, dest, cols, seg, recv_sem, pass_sem, far_sem):
    pc = mv.place
    for c in range(2):
        mv.landed(dest.at[span((2 * pc.q + c) * size, size), cols], recv_sem.at[seg, c])
    both = dest.at[span(2 * pc.q * size, 2 * size), cols]
    if pc.quads == 4:
        for j, quad in enumerate(pc.quad_pair()[:2]):
            mv.send(both, both, pass_sem.at[seg, j], far_sem.at[seg, j], pc.in_quad(quad))
        return
    for j in range(1, pc.quads):
        other = pc.in_quad(pc.across(j))
        mv.send(both, both, pass_sem.at[seg, j - 1], far_sem.at[seg, pc.quads - j - 1], other)


def weights_relay(mv, size, dest, cols, seg, pass_sem, far_sem):
    pc = mv.place
    if pc.quads != 4:
        return
    quads = pc.quad_pair()
    for j in range(2):
        mv.landed(dest.at[span(2 * quads[j] * size, 2 * size), cols], far_sem.at[seg, j])
        part = dest.at[span((2 * quads[j] + j) * size, size), cols]
        mv.send(part, part, pass_sem.at[seg, 2 + j], far_sem.at[seg, 2 + j], pc.in_quad(quads[1 - j]))


def weights_in(mv, size, dest, cols, seg, far_sem):
    pc = mv.place
    if pc.quads == 4:
        for j in range(2):
            part = dest.at[span((2 * pc.quad_pair()[2] + j) * size, size), cols]
            mv.landed(part, far_sem.at[seg, 2 + j])
        return
    for j in range(1, pc.quads):
        part = dest.at[span(2 * pc.across(j) * size, 2 * size), cols]
        mv.landed(part, far_sem.at[seg, j - 1])


def over_tiles(width, body, most=256):
    tile = min(most, width)

    def step(i, carry):
        body(span(i * tile, tile))
        return carry

    lax.fori_loop(0, width // tile, step, 0)


def reduce_rows(mv, s, sems, own, width, partial):
    pc = mv.place
    size = own // CHUNKS
    send_a, recv_a, send_z, recv_z = sems
    order = list(range(1, pc.half)) + [0]
    mark = len(mv.open)
    for j in order:
        block = (1 - pc.c) * pc.half + pc.along(j)

        def give(tile, j=j, block=block):
            s.core_out[j, :, tile] = partial(block, tile).astype(jnp.bfloat16)

        over_tiles(width, give)
        mv.send(s.core_out.at[j], s.core_in.at[j], send_a.at[j], recv_a.at[j], pc.beside())
    for j in order:
        block = pc.c * pc.half + pc.along(j)
        mv.landed(s.core_in.at[j], recv_a.at[j])
        if j:

            def add(tile, j=j, block=block):
                total = partial(block, tile) + s.core_in[j, :, tile].astype(jnp.float32)
                s.chip_out[j - 1, :, tile] = total.astype(jnp.bfloat16)

            over_tiles(width, add)
            other = pc.at(pc.q, pc.c, pc.h, pc.along(j))
            for k in range(CHUNKS):
                rows = pl.ds(k * size, size)
                mv.send(
                    s.chip_out.at[j - 1, rows],
                    s.chip_in.at[pc.half - j - 1, rows],
                    send_z.at[j, k],
                    recv_z.at[pc.half - j, k],
                    other,
                )
        else:

            def hold(tile, block=block):
                total = partial(block, tile) + s.core_in[0, :, tile].astype(jnp.float32)
                s.held[:, tile] = total

            over_tiles(width, hold)
    return mv.since(mark)


def reduced_chunk(mv, s, sems, own, k):
    pc = mv.place
    size = own // CHUNKS
    rows = pl.ds(k * size, size)
    total = s.held[rows, :]
    for j in range(1, pc.half):
        mv.landed(s.chip_in.at[j - 1, rows], sems[3].at[j, k])
        total = total + s.chip_in[j - 1, rows, :].astype(jnp.float32)
    return total


def in_order(mv, buf, own, pass_sem, recv_sem, work, between=None):
    pc = mv.place
    for j in range(pc.half):
        if j:
            for k in range(CHUNKS):
                rows_pass(mv, buf, own, j, k, pass_sem, recv_sem)
        work(pc.c * pc.half + pc.along(j))
        for k in range(CHUNKS):
            rows_in(mv, buf, own, j, k, recv_sem)
        work((1 - pc.c) * pc.half + pc.along(j))
        if j == 0 and between is not None:
            between()


def to_group(mv, own, source, target, send_sem, recv_sem):
    pc = mv.place
    size = pc.tensor_size
    for j in range(1, size):
        rank = lax.rem(pc.rank + j, size)
        other = pc.at(pc.q, lax.div(rank, pc.half), pc.h, lax.rem(rank, pc.half))
        mv.send(source(rank), target, send_sem.at[j], recv_sem.at[size - j], other)


def grad_out(mv, s, shard, start, width, left, right, seg):
    pc = mv.place

    def rows_of(quad):
        return span(2 * shard * quad, 2 * shard)

    def fill_rows(rows):
        def fill(tile):
            tile_at = pl.ds(pl.multiple_of(start + tile.start, tile.size), tile.size)
            s.grads[rows, tile_at] = dense_tn(left(rows), right(tile)).astype(jnp.bfloat16)

        over_tiles(width, fill)

    if pc.quads == 4:
        quads = pc.quad_pair()
        fill_rows(rows_of(quads[2]))
        for way in range(2):
            cols = pl.ds(start + way * (width // 2), width // 2)
            fill_rows(rows_of(quads[way]))
            for slot, quad in ((1, quads[2]), (0, quads[way])):
                mv.send(
                    s.grads.at[rows_of(quad), cols],
                    s.grads_in.at[slot, :, cols],
                    s.grad_send.at[seg, 2 * way + slot],
                    s.grad_recv.at[seg, 2 * way + slot],
                    pc.in_quad(quads[way]),
                )
        fill_rows(rows_of(pc.q))
        return
    cols = pl.ds(start, width)
    for at in range(0, s.grads.shape[0], 128):
        fill_rows(pl.ds(at, 128))
    for j in range(1, pc.quads):
        quad = pc.across(j)
        mv.send(
            s.grads.at[rows_of(quad), cols],
            s.grads_in.at[pc.quads - j - 1, :, cols],
            s.grad_send.at[seg, j],
            s.grad_recv.at[seg, pc.quads - j],
            pc.in_quad(quad),
        )


def grad_pass(mv, s, shard, start, width, seg):
    pc = mv.place
    if pc.quads != 4:
        return
    quads = pc.quad_pair()
    for way in range(2):
        at = start + way * (width // 2)
        cols = pl.ds(at, width // 2)
        other = quads[1 - way]
        rows = span(2 * shard * other, 2 * shard)
        mv.landed(s.grads_in.at[1, :, cols], s.grad_recv.at[seg, 2 * way + 1])

        def add(tile, at=at, rows=rows):
            tile_at = pl.ds(pl.multiple_of(at + tile.start, 128), tile.size)
            value = s.grads[rows, tile_at].astype(jnp.float32) + s.grads_in[1, :, tile_at].astype(jnp.float32)
            s.grads[rows, tile_at] = value.astype(jnp.bfloat16)

        over_tiles(width // 2, add, 128)
        mv.send(
            s.grads.at[rows, cols],
            s.grads_in.at[2, :, cols],
            s.grad_send.at[seg, 4 + way],
            s.grad_recv.at[seg, 4 + way],
            pc.in_quad(other),
        )


def grad_sum(mv, s, shard, start, width, seg, result):
    pc = mv.place
    cols = pl.ds(start, width)
    if pc.quads == 4:
        for way in range(2):
            part = pl.ds(start + way * (width // 2), width // 2)
            mv.landed(s.grads_in.at[0, :, part], s.grad_recv.at[seg, 2 * way])
            mv.landed(s.grads_in.at[2, :, part], s.grad_recv.at[seg, 4 + way])
        slots = (0, 2)
    else:
        for j in range(1, pc.quads):
            mv.landed(s.grads_in.at[j - 1, :, cols], s.grad_recv.at[seg, j])
        slots = tuple(range(pc.quads - 1))

    def total(tile):
        tile_at = pl.ds(pl.multiple_of(start + tile.start, tile.size), tile.size)
        value = s.grads[span(2 * shard * pc.q, 2 * shard), tile_at].astype(jnp.float32)
        for slot in slots:
            value = value + s.grads_in[slot, :, tile_at].astype(jnp.float32)
        s.grads_out[:, tile_at] = value.astype(jnp.bfloat16)

    over_tiles(width, total)
    for core in range(2):
        mv.keep_or_send(
            s.grads_out.at[pl.ds(core * shard, shard), cols],
            result.at[pc.h, :, cols],
            s.owner_send.at[seg, core],
            s.owner_recv.at[seg, pc.h],
            pc.at(pc.q, core, pc.c, pc.l),
            jnp.logical_and(pc.stays, pc.c == core),
        )


def layer_kernel(names, *refs):
    by_name = dict(zip(names, refs))
    s = types.SimpleNamespace(**by_name)
    sems_ra = (s.ra_send_a, s.ra_recv_a, s.ra_send_z, s.ra_recv_z)
    sems_rb = (s.rb_send_a, s.rb_recv_a, s.rb_send_z, s.rb_recv_z)
    sems_rc = (s.rc_send_a, s.rc_recv_a, s.rc_send_z, s.rc_recv_z)
    pc = Place()
    mv = Mover(pc)
    seq, wide = s.seq, s.wide
    own = s.x.shape[0]
    size = own // CHUNKS
    total_rows, width = seq.shape
    heads = wide.shape[1] // 3
    hidden = s.inner.shape[1] // 2
    shard = s.key_part.shape[0]
    group = pc.tensor_size
    pairs = heads // PAIR
    mine = span(pc.rank * own, own)
    vec, sums = s.vec, s.sums
    f32 = jnp.float32
    inner, hid_cols, out_cols = s.inner, pl.ds(0, hidden), pl.ds(hidden, hidden)
    scale = HEAD_DIM ** (-0.5)

    def block_rows(block):
        return span(block * own, own)

    def own_chunk(k):
        return span(pc.rank * own + k * size, size)

    new_rank = pc.h * pc.half + pc.l
    new_out = s.out_all.at[span(new_rank * width, width)]
    my_out = s.out_all.at[span(pc.rank * width, width)]
    parts = (
        (s.out_turned, new_out, my_out, pl.ds(0, heads)),
        (s.inner_part, inner, inner, hid_cols),
        (s.outer_turned, inner, inner, out_cols),
        (s.query_part, wide, wide, pl.ds(0, heads)),
        (s.key_part, wide, wide, pl.ds(heads, heads)),
        (s.value_part, wide, wide, pl.ds(2 * heads, heads)),
    )
    attn_parts = (3, 4, 5)

    def start_weight(seg):
        source, target, _, cols = parts[seg]
        place = span((2 * pc.q + pc.c) * shard, shard)
        for half in range(2):
            mv.keep_or_send(
                source,
                target.at[place, cols],
                s.w_send.at[seg, half],
                s.w_recv.at[seg, pc.c],
                pc.at(pc.q, pc.h, half, pc.l),
                jnp.logical_and(pc.stays, pc.h == half),
            )

    def pass_weight(seg):
        weights_pass(mv, shard, parts[seg][2], parts[seg][3], seg, s.w_recv, s.w_pass, s.w_far)

    def relay_weight(seg):
        weights_relay(mv, shard, parts[seg][2], parts[seg][3], seg, s.w_pass, s.w_far)

    def end_weight(seg):
        weights_in(mv, shard, parts[seg][2], parts[seg][3], seg, s.w_far)

    pc.greet()
    column_size = 2 * group
    every = s.every
    spot = (2 * pc.q + pc.c) * group + pc.h * pc.half + pc.l
    keep = pltpu.make_async_copy(s.vectors, every.at[spot], s.v_recv.at[0])
    keep.start()
    for j in range(1, column_size):
        mv.send(s.vectors, every.at[spot], s.v_send.at[j], s.v_recv.at[column_size - j], pc.column_peer(j)[1])
    for seg in attn_parts:
        start_weight(seg)
    s.out_turned[...] = jnp.transpose(s.out_part[...])
    s.outer_turned[...] = jnp.transpose(s.outer_part[...])
    sums[...] = jnp.zeros_like(sums)
    keep.wait()
    for j in range(1, column_size):
        mv.landed(every.at[spot], s.v_recv.at[j])
    column = every.at[span(2 * pc.q * group, column_size)]
    for j in range(1, pc.quads):
        mv.send(column, column, s.v_pass.at[j], s.v_far.at[pc.quads - j], pc.in_quad(pc.across(j)))
    for seg in attn_parts:
        pass_weight(seg)
    for k in range(CHUNKS):
        mv.keep_or_send(
            s.x.at[pl.ds(k * size, size)],
            seq.at[span(new_rank * own + k * size, size)],
            s.swap_send.at[k],
            s.swap_recv.at[k],
            pc.swapped(),
            pc.stays,
        )
    start_weight(0)
    for j in range(1, pc.quads):
        mv.landed(column, s.v_far.at[j])
    piece = width // (pc.dp_size * group)
    vec[...] = jnp.zeros_like(vec)
    for i in range(pc.dp_size * group):
        vec[0:6, i * piece : (i + 1) * piece] = every[i, 0:6, 0:piece]
    qv_piece, in_piece = heads // pc.dp_size, hidden // pc.dp_size
    for i in range(pc.dp_size):
        held = every[i * group + pc.rank]
        for part in range(2):
            vec[6:7, part * heads + i * qv_piece : part * heads + (i + 1) * qv_piece] = (
                held[6:7, part * qv_piece : (part + 1) * qv_piece]
            )
        vec[7:8, i * in_piece : (i + 1) * in_piece] = held[7:8, 0:in_piece]
    length = every[(2 * pc.q + pc.h) * group][6:7, 127:128]
    for k in range(CHUNKS):
        mv.landed(seq.at[own_chunk(k)], s.swap_recv.at[k])
        rows_out(mv, seq, own, k, s.row_send, s.row_recv)
        if k == CHUNKS - 2:
            for seg in attn_parts:
                relay_weight(seg)
    for j in range(1, pc.half):
        for k in range(CHUNKS):
            rows_pass(mv, seq, own, j, k, s.row_pass, s.row_recv)
    pass_weight(0)
    start_weight(1)
    for j in range(pc.half):
        for k in range(CHUNKS):
            rows_in(mv, seq, own, j, k, s.row_recv)
    for seg in attn_parts:
        end_weight(seg)
    relay_weight(0)

    big = min(512, total_rows)
    qkv = s.qkv

    def project(i, carry):
        rows = span(i * big, big)
        query = (dense(seq[rows, :], wide[:, 0:heads]) + vec[6:7, 0:heads]).astype(jnp.bfloat16)
        qkv[rows, 0:heads] = (query.astype(f32) * scale).astype(jnp.bfloat16)
        qkv[rows, heads : 2 * heads] = dense(seq[rows, :], wide[:, heads : 2 * heads]).astype(jnp.bfloat16)
        value = dense(seq[rows, :], wide[:, 2 * heads : 3 * heads]) + vec[6:7, heads : 2 * heads]
        qkv[rows, 2 * heads : 3 * heads] = value.astype(jnp.bfloat16)
        return carry

    lax.fori_loop(0, total_rows // big, project, 0)
    end_weight(0)
    for k in range(CHUNKS):
        rows_out(mv, s.out_all, width, k, s.out_send, s.out_recv)

    step_rows = min(256, total_rows)
    spot = lax.broadcasted_iota(jnp.int32, (1, total_rows), 1).astype(f32)
    bias = jnp.where(spot < length, 0.0, -jnp.inf).astype(f32)

    def head_cols(pair, head, part):
        start = part * heads + pair * PAIR + head * HEAD_DIM
        return slice(start, start + HEAD_DIM)

    for pair in range(pairs):

        def attend(i, carry, pair=pair):
            rows = span(i * step_rows, step_rows)
            found = []
            for head in range(2):
                scores = dense_nt(qkv[rows, head_cols(pair, head, 0)], qkv[:, head_cols(pair, head, 1)]) + bias
                top = jnp.max(scores, axis=-1, keepdims=True)
                grown = jnp.exp(scores - top)
                total = jnp.sum(grown, axis=-1, keepdims=True)
                probs = (grown * (1.0 / total)).astype(jnp.bfloat16)
                lane = 2 * pair + head
                s.log_total[rows, lane : lane + 1] = top + jnp.log(total)
                found.append(dense(probs, qkv[:, head_cols(pair, head, 2)]))
            s.ctx[rows, pair * PAIR : (pair + 1) * PAIR] = jnp.concatenate(found, axis=1).astype(jnp.bfloat16)
            return carry

        lax.fori_loop(0, total_rows // step_rows, attend, 0)
        place = span(pc.rank * heads + pair * PAIR, PAIR)
        pair_cols = pl.ds(pair * PAIR, PAIR)
        to_group(
            mv, own,
            lambda rank, cols=pair_cols: s.ctx.at[span(rank * own, own), cols],
            s.own_ctx.at[:, place],
            s.ctx_send.at[pair], s.ctx_recv.at[pair],
        )
        s.own_ctx[:, place] = s.ctx[mine, pair_cols]
        if pair == 0:
            for j in range(1, pc.half):
                for k in range(CHUNKS):
                    rows_pass(mv, s.out_all, width, j, k, s.out_pass, s.out_recv)
            pass_weight(1)
            start_weight(2)
    mv.keep_or_send(s.cot, s.cot_in, s.cot_send.at[0], s.cot_recv.at[0], pc.swapped(), pc.stays)
    for pair in range(pairs):
        for j in range(1, group):
            mv.landed(s.own_ctx.at[:, pl.ds(0, PAIR)], s.ctx_recv.at[pair, j])
    relay_weight(1)
    pass_weight(2)
    for j in range(pc.half):
        for k in range(CHUNKS):
            rows_in(mv, s.out_all, width, j, k, s.out_recv)

    for k in range(CHUNKS):
        rows = pl.ds(k * size, size)
        total = seq[own_chunk(k), :].astype(f32) + vec[0:1, :]
        for t in range(group):
            total = total + dense_nt(
                s.own_ctx[rows, t * heads : (t + 1) * heads], s.out_all[t * width : (t + 1) * width, :]
            )
        s.resid[rows, :] = total
        normed, _ = norm_parts(total)
        middle = normed * vec[1:2, :] + vec[2:3, :]
        s.middle[rows, :] = middle
        s.mid_rows[own_chunk(k), :] = middle.astype(jnp.bfloat16)
        rows_out(mv, s.mid_rows, own, k, s.mid_send, s.mid_recv)

    end_weight(1)

    def expand(block):
        rows = block_rows(block)

        def one(tile):
            pre = dense(s.mid_rows[rows, :], inner[:, tile]) + vec[7:8, tile]
            cdf = 0.5 * (1.0 + lax.erf(pre * inv_root2))
            s.hid[rows, tile] = (pre * cdf).astype(jnp.bfloat16)
            s.slope[rows, tile] = cdf + pre * inv_root2pi * jnp.exp(-0.5 * pre * pre)

        over_tiles(hidden, one)

    in_order(mv, s.mid_rows, own, s.mid_pass, s.mid_recv, expand, lambda: relay_weight(2))
    end_weight(2)
    sent_ra = reduce_rows(
        mv, s, sems_ra, own, width,
        lambda block, tile: dense_nt(s.hid[block_rows(block), :], inner[tile, out_cols]),
    )
    mv.landed(s.cot_in, s.cot_recv.at[0])
    for k in range(CHUNKS):
        rows = pl.ds(k * size, size)
        total = s.middle[rows, :] + reduced_chunk(mv, s, sems_ra, own, k) + vec[3:4, :]
        normed, inverse = norm_parts(total)
        up = s.cot_in[rows, :].astype(f32)
        d_resid = norm_back(normed, inverse, vec[4:5, :], up)
        s.d_resid[rows, :] = d_resid
        s.ffn_rows[own_chunk(k), :] = d_resid.astype(jnp.bfloat16)
        rows_out(mv, s.ffn_rows, own, k, s.ffn_send, s.ffn_recv)
        sums[3:4, :] += jnp.sum(d_resid, axis=0, keepdims=True)
        sums[4:5, :] += jnp.sum(up * normed, axis=0, keepdims=True)
        sums[5:6, :] += jnp.sum(up, axis=0, keepdims=True)
        s.out_stage[rows, :] = (normed * vec[4:5, :] + vec[5:6, :]).astype(jnp.bfloat16)

    mv.finish(sent_ra)

    def shrink(block):
        rows = block_rows(block)

        def one(tile):
            shifted = pl.ds(pl.multiple_of(hidden + tile.start, tile.size), tile.size)
            d_pre = dense(s.ffn_rows[rows, :], inner[:, shifted]) * s.slope[rows, tile]
            sums[7:8, tile] += jnp.sum(d_pre, axis=0, keepdims=True)
            s.d_pre[rows, tile] = d_pre.astype(jnp.bfloat16)

        over_tiles(hidden, one)

    in_order(mv, s.ffn_rows, own, s.ffn_pass, s.ffn_recv, shrink)
    sent_rb = reduce_rows(
        mv, s, sems_rb, own, width,
        lambda block, tile: dense_nt(s.d_pre[block_rows(block), :], inner[tile, hid_cols]),
    )
    for k in range(CHUNKS):
        rows = pl.ds(k * size, size)
        mv.keep_or_send(
            s.out_stage.at[rows], s.block_out.at[rows],
            s.bo_send.at[k], s.bo_recv.at[k], pc.swapped(), pc.stays,
        )
    at_out, at_in, at_outer = 3 * heads, 4 * heads, 4 * heads + hidden
    grad_out(
        mv, s, shard, at_outer, hidden,
        lambda rows: s.ffn_rows[:, rows], lambda tile: s.hid[:, tile], 0,
    )
    grad_out(
        mv, s, shard, at_in, hidden,
        lambda rows: s.mid_rows[:, rows], lambda tile: s.d_pre[:, tile], 1,
    )
    for k in range(CHUNKS):
        rows = pl.ds(k * size, size)
        up = reduced_chunk(mv, s, sems_rb, own, k) + s.d_resid[rows, :]
        normed, inverse = norm_parts(s.resid[rows, :])
        d_resid = norm_back(normed, inverse, vec[1:2, :], up)
        s.d_resid[rows, :] = d_resid
        s.attn_rows[own_chunk(k), :] = d_resid.astype(jnp.bfloat16)
        sums[0:1, :] += jnp.sum(d_resid, axis=0, keepdims=True)
        sums[1:2, :] += jnp.sum(up * normed, axis=0, keepdims=True)
        sums[2:3, :] += jnp.sum(up, axis=0, keepdims=True)

    mv.finish(sent_rb)

    for t in range(group):
        s.d_ctx_out[t, :, :] = dense(
            s.attn_rows[mine, :], s.out_all[t * width : (t + 1) * width, :]
        ).astype(jnp.bfloat16)
    to_group(
        mv, own,
        lambda rank: s.d_ctx_out.at[rank],
        s.d_ctx.at[mine],
        s.d_ctx_send, s.d_ctx_recv,
    )
    s.d_ctx[mine, :] = s.d_ctx_out[pc.rank, :, :]
    for k in range(CHUNKS):
        rows_out(mv, s.attn_rows, own, k, s.at_send, s.at_recv)
    for j in range(1, group):
        mv.landed(s.d_ctx.at[mine], s.d_ctx_recv.at[j])
    d_qkv = s.d_qkv
    grad_pass(mv, s, shard, at_outer, hidden, 0)
    for pair in range(pairs):
        s.key_sum[...] = jnp.zeros_like(s.key_sum)
        s.value_sum[...] = jnp.zeros_like(s.value_sum)

        def attend_back(i, carry, pair=pair):
            rows = span(i * step_rows, step_rows)
            found = []
            for head in range(2):
                cols = slice(head * HEAD_DIM, (head + 1) * HEAD_DIM)
                lane = 2 * pair + head
                query, key = qkv[rows, head_cols(pair, head, 0)], qkv[:, head_cols(pair, head, 1)]
                grad = s.d_ctx[rows, head_cols(pair, head, 0)]
                scores = dense_nt(query, key) + bias
                probs = jnp.exp(scores - s.log_total[rows, lane : lane + 1])
                d_probs = dense_nt(grad, qkv[:, head_cols(pair, head, 2)])
                within = jnp.sum(probs * d_probs, axis=-1, keepdims=True)
                d_scores = (probs * (d_probs - within)).astype(jnp.bfloat16)
                found.append(dense(d_scores, key) * scale)
                s.value_sum[cols, :] += dense_tn(grad, probs.astype(jnp.bfloat16))
                s.key_sum[cols, :] += dense_tn(query, d_scores)
            d_query = jnp.concatenate(found, axis=1)
            d_qkv[rows, pair * PAIR : (pair + 1) * PAIR] = d_query.astype(jnp.bfloat16)
            sums[6:7, pair * PAIR : (pair + 1) * PAIR] += jnp.sum(d_query, axis=0, keepdims=True)
            return carry

        lax.fori_loop(0, total_rows // step_rows, attend_back, 0)
        at_key = slice(heads + pair * PAIR, heads + (pair + 1) * PAIR)
        at_value = slice(2 * heads + pair * PAIR, 2 * heads + (pair + 1) * PAIR)
        d_qkv[:, at_key] = jnp.transpose(s.key_sum[...]).astype(jnp.bfloat16)
        d_value = jnp.transpose(s.value_sum[...])
        d_qkv[:, at_value] = d_value.astype(jnp.bfloat16)
        sums[6:7, at_key] = jnp.sum(d_value, axis=0, keepdims=True)
        if pair == 0:
            grad_sum(mv, s, shard, at_outer, hidden, 0, s.weight_grads)
            grad_pass(mv, s, shard, at_in, hidden, 1)
            for j in range(1, pc.half):
                for k in range(CHUNKS):
                    rows_pass(mv, s.attn_rows, own, j, k, s.at_pass, s.at_recv)
            for j in range(pc.half):
                for k in range(CHUNKS):
                    rows_in(mv, s.attn_rows, own, j, k, s.at_recv)
            grad_out(
                mv, s, shard, at_out, heads,
                lambda rows: s.attn_rows[:, rows], lambda tile: s.ctx[:, tile], 2,
            )
    grad_sum(mv, s, shard, at_in, hidden, 1, s.weight_grads)
    grad_pass(mv, s, shard, at_out, heads, 2)
    slots = s.sum_slots
    slots[pc.column] = sums[...]
    for j in range(1, 2 * group):
        mv.send(
            sums, slots.at[pc.column],
            s.sum_send.at[j], s.sum_recv.at[2 * group - j], pc.column_peer(j)[1],
        )
    grad_out(
        mv, s, shard, 0, 3 * heads,
        lambda rows: seq[:, rows], lambda tile: d_qkv[:, tile], 3,
    )
    sent_rc = reduce_rows(
        mv, s, sems_rc, own, width,
        lambda block, tile: dense_nt(d_qkv[block_rows(block), :], wide[tile, :]),
    )
    grad_sum(mv, s, shard, at_out, heads, 2, s.weight_grads)
    for k in range(CHUNKS):
        if k == CHUNKS // 2:
            grad_pass(mv, s, shard, 0, 3 * heads, 3)
        rows = pl.ds(k * size, size)
        s.ig_stage[rows, :] = (reduced_chunk(mv, s, sems_rc, own, k) + s.d_resid[rows, :]).astype(jnp.bfloat16)
        mv.keep_or_send(
            s.ig_stage.at[rows], s.input_grad.at[rows],
            s.ig_send.at[k], s.ig_recv.at[k], pc.swapped(), pc.stays,
        )
    mv.finish(sent_rc)
    for j in range(1, 2 * group):
        mv.landed(slots.at[0], s.sum_recv.at[j])
    whole = slots[0]
    for j in range(1, 2 * group):
        whole = whole + slots[j]
    chosen = pc.h * group + pc.l
    biases = slots[chosen] + slots[chosen + pc.half]
    row = lax.broadcasted_iota(jnp.int32, whole.shape, 0)
    summed = jnp.where(row < 6, whole, biases)
    s.sum_stage[...] = summed
    for j in range(1, pc.quads):
        other = pc.at(pc.across(j), pc.c, pc.h, pc.l)
        mv.send(s.sum_stage, s.sum_far.at[pc.quads - j - 1], s.far_send.at[j], s.far_recv.at[pc.quads - j], other)
    for j in range(1, pc.quads):
        mv.landed(s.sum_stage, s.far_recv.at[j])
        summed = summed + s.sum_far[j - 1]
    s.vec_grads[...] = summed
    grad_sum(mv, s, shard, 0, 3 * heads, 3, s.weight_grads)
    for k in range(CHUNKS):
        rows = pl.ds(k * size, size)
        mv.landed(s.block_out.at[rows], s.bo_recv.at[k])
        mv.landed(s.input_grad.at[rows], s.ig_recv.at[k])
    for seg, (start, count) in enumerate(
        ((at_outer, hidden), (at_in, hidden), (at_out, heads), (0, 3 * heads))
    ):
        for h in range(2):
            mv.landed(s.weight_grads.at[h, :, pl.ds(start, count)], s.owner_recv.at[seg, h])
    mv.close()


def run_layer(x, query_part, key_part, value_part, out_part, inner_part, outer_part, vectors, cot):
    dp_size, tensor_size = lax.axis_size("dp"), lax.axis_size("tensor")
    quads, half = dp_size // 2, tensor_size // 2
    own, width = x.shape
    rows = own * tensor_size
    shard, heads = query_part.shape
    hidden = inner_part.shape[1]
    pairs = heads // PAIR
    every = 4 * heads + 2 * hidden
    bf16, f32 = jnp.bfloat16, jnp.float32
    ins = dict(
        x=x, query_part=query_part, key_part=key_part, value_part=value_part, inner_part=inner_part,
        vectors=vectors, cot=cot, out_part=out_part, outer_part=outer_part,
    )
    outs = dict(
        block_out=((own, width), bf16),
        input_grad=((own, width), bf16),
        weight_grads=((2, shard, every), bf16),
        vec_grads=((8, width), f32),
    )
    buffers = dict(
        seq=((rows, width), bf16),
        wide=((width, 3 * heads), bf16),
        vec=((8, width), f32),
        every=((dp_size * tensor_size,) + vectors.shape, f32),
        out_turned=((shard, heads), bf16),
        outer_turned=((shard, hidden), bf16),
        inner=((width, 2 * hidden), bf16),
        out_all=((tensor_size * width, heads), bf16),
        qkv=((rows, 3 * heads), bf16),
        log_total=((rows, 128), f32),
        ctx=((rows, heads), bf16),
        own_ctx=((own, width), bf16),
        resid=((own, width), f32),
        middle=((own, width), f32),
        d_resid=((own, width), f32),
        held=((own, width), f32),
        mid_rows=((rows, width), bf16),
        slope=((rows, hidden), f32),
        hid=((rows, hidden), bf16),
        ffn_rows=((rows, width), bf16),
        d_pre=((rows, hidden), bf16),
        attn_rows=((rows, width), bf16),
        d_ctx_out=((tensor_size, own, heads), bf16),
        d_ctx=((rows, heads), bf16),
        d_qkv=((rows, 3 * heads), bf16),
        key_sum=((PAIR, rows), f32),
        value_sum=((PAIR, rows), f32),
        core_out=((half, own, width), bf16),
        core_in=((half, own, width), bf16),
        chip_out=((half - 1, own, width), bf16),
        chip_in=((half - 1, own, width), bf16),
        grads=((width, every), bf16),
        grads_in=((quads - 1, 2 * shard, every), bf16),
        grads_out=((2 * shard, every), bf16),
        cot_in=((own, width), bf16),
        out_stage=((own, width), bf16),
        ig_stage=((own, width), bf16),
        sums=((8, width), f32),
        sum_slots=((2 * tensor_size, 8, width), f32),
        sum_stage=((8, width), f32),
        sum_far=((quads - 1, 8, width), f32),
    )
    sems = dict(
        w_send=(6, 2), w_recv=(6, 2), w_pass=(6, quads), w_far=(6, quads),
        swap_send=(CHUNKS,), swap_recv=(CHUNKS,),
        v_send=(2 * tensor_size,), v_recv=(2 * tensor_size,), v_pass=(quads,), v_far=(quads,),
        cot_send=(1,), cot_recv=(1,),
        ctx_send=(pairs, tensor_size), ctx_recv=(pairs, tensor_size),
        d_ctx_send=(tensor_size,), d_ctx_recv=(tensor_size,),
        bo_send=(CHUNKS,), bo_recv=(CHUNKS,), ig_send=(CHUNKS,), ig_recv=(CHUNKS,),
        grad_send=(4, quads + 2), grad_recv=(4, quads + 2), owner_send=(4, 2), owner_recv=(4, 2),
        sum_send=(2 * tensor_size,), sum_recv=(2 * tensor_size,), far_send=(quads,), far_recv=(quads,),
    )
    for tag in ("row", "out", "mid", "ffn", "at"):
        sems[tag + "_send"] = (CHUNKS, half)
        sems[tag + "_recv"] = (tensor_size, CHUNKS)
        sems[tag + "_pass"] = (CHUNKS, half)
    for tag in ("ra", "rb", "rc"):
        sems[tag + "_send_a"] = (half,)
        sems[tag + "_recv_a"] = (half,)
        sems[tag + "_send_z"] = (half, CHUNKS)
        sems[tag + "_recv_z"] = (half, CHUNKS)
    names = tuple(ins) + tuple(outs) + tuple(buffers) + tuple(sems)
    vmem, anywhere = pl.BlockSpec(memory_space=pltpu.VMEM), pl.BlockSpec(memory_space=pl.ANY)
    return pl.pallas_call(
        functools.partial(layer_kernel, names),
        out_shape=[jax.ShapeDtypeStruct(shape, kind) for shape, kind in outs.values()],
        in_specs=[anywhere] * 7 + [vmem] * 2,
        out_specs=[vmem] * len(outs),
        scratch_shapes=[pltpu.VMEM(shape, kind) for shape, kind in buffers.values()]
        + [pltpu.SemaphoreType.DMA(shape) for shape in sems.values()],
        compiler_params=pltpu.CompilerParams(
            collective_id=0, has_side_effects=True, vmem_limit_bytes=VMEM_LIMIT
        ),
        name="layer",
    )(*ins.values())


def finish_kernel(cuts, block_ref, input_ref, grads_ref, out_block, out_input, *out_grads):
    out_block[...] = block_ref[...]
    out_input[...] = input_ref[...].astype(jnp.float32)
    for i, out in enumerate(out_grads):
        cols = slice(cuts[i], cuts[i + 1])
        total = grads_ref[0, :, cols].astype(jnp.float32) + grads_ref[1, :, cols].astype(jnp.float32)
        out[...] = total if out.shape == total.shape else jnp.transpose(total)


def finish(block_out, input_grad, weight_grads, shapes):
    cuts = [0]
    for shape, turned in shapes:
        cuts.append(cuts[-1] + (shape[0] if turned else shape[1]))
    f32 = jnp.float32
    return pl.pallas_call(
        functools.partial(finish_kernel, cuts),
        out_shape=[
            jax.ShapeDtypeStruct(block_out.shape, block_out.dtype),
            jax.ShapeDtypeStruct(input_grad.shape, f32),
        ]
        + [jax.ShapeDtypeStruct(shape, f32) for shape, _ in shapes],
        compiler_params=pltpu.CompilerParams(vmem_limit_bytes=32 << 20),
        name="finish",
    )(block_out, input_grad, weight_grads)


def per_device(
    block_input,
    lengths,
    query_weight,
    key_weight,
    value_weight,
    query_bias,
    value_bias,
    output_weight,
    output_bias,
    first_gain,
    first_shift,
    inner_weight,
    inner_bias,
    outer_weight,
    outer_bias,
    second_gain,
    second_shift,
    cotangent,
):
    f32 = jnp.float32
    dp_size, tensor_size = lax.axis_size("dp"), lax.axis_size("tensor")
    dp, tensor = lax.axis_index("dp"), lax.axis_index("tensor")

    features = (output_bias, first_gain, first_shift, outer_bias, second_gain, second_shift)
    biases = (query_bias, value_bias, inner_bias)
    def lanes(row):
        return jnp.pad(row, ((0, 0), (0, 128 - row.shape[1])))

    query_bias, value_bias, inner_bias = (bias.astype(f32)[None] for bias in biases)
    mixed = jnp.concatenate([query_bias, value_bias], axis=1)
    length = jnp.broadcast_to(lengths.astype(f32)[None], (1, 128 - mixed.shape[1]))
    vectors = jnp.concatenate(
        [lanes(jnp.stack(features)), jnp.concatenate([mixed, length], axis=1), lanes(inner_bias)]
    )
    block_out, input_grad, weight_grads, vec_grads = run_layer(
        block_input, query_weight, key_weight, value_weight, output_weight, inner_weight, outer_weight,
        vectors, cotangent,
    )

    width = block_input.shape[1]
    heads, hidden = query_weight.shape[1], inner_weight.shape[1]
    block_out, input_grad, *pieces = finish(
        block_out, input_grad, weight_grads,
        (
            (query_weight.shape, False),
            (key_weight.shape, False),
            (value_weight.shape, False),
            (output_weight.shape, True),
            (inner_weight.shape, False),
            (outer_weight.shape, True),
        ),
    )
    piece = width // (dp_size * tensor_size)
    mine = lax.dynamic_slice_in_dim(vec_grads, (dp * tensor_size + tensor) * piece, piece, axis=1)

    def bias_piece(row, start, count):
        size = count // dp_size
        return lax.dynamic_slice(vec_grads, (row, start + dp * size), (1, size))[0]

    return (
        block_out,
        input_grad,
        pieces[0],
        pieces[1],
        pieces[2],
        bias_piece(6, 0, heads),
        bias_piece(6, heads, heads),
        pieces[3],
        mine[0],
        mine[1],
        mine[2],
        pieces[4],
        bias_piece(7, 0, hidden),
        pieces[5],
        mine[3],
        mine[4],
        mine[5],
    )


def solution(mesh):
    return jax.shard_map(
        per_device,
        mesh=mesh,
        in_specs=(
            P(("dp", "tensor"), None),
            P("dp"),
            P("dp", "tensor"),
            P("dp", "tensor"),
            P("dp", "tensor"),
            P(("tensor", "dp")),
            P(("tensor", "dp")),
            P("tensor", "dp"),
            P(("dp", "tensor")),
            P(("dp", "tensor")),
            P(("dp", "tensor")),
            P("dp", "tensor"),
            P(("tensor", "dp")),
            P("tensor", "dp"),
            P(("dp", "tensor")),
            P(("dp", "tensor")),
            P(("dp", "tensor")),
            P(("dp", "tensor"), None),
        ),
        out_specs=(
            P(("dp", "tensor"), None),
            P(("dp", "tensor"), None),
            P("dp", "tensor"),
            P("dp", "tensor"),
            P("dp", "tensor"),
            P(("tensor", "dp")),
            P(("tensor", "dp")),
            P("tensor", "dp"),
            P(("dp", "tensor")),
            P(("dp", "tensor")),
            P(("dp", "tensor")),
            P("dp", "tensor"),
            P(("tensor", "dp")),
            P("tensor", "dp"),
            P(("dp", "tensor")),
            P(("dp", "tensor")),
            P(("dp", "tensor")),
        ),
        check_vma=False,
    )
```

```python
import functools
import types

import jax
import jax.numpy as jnp
from jax import lax
from jax.experimental import pallas as pl
from jax.experimental.pallas import tpu as pltpu
from jax.sharding import PartitionSpec as P

HEAD_DIM = 64
PAIR = 2 * HEAD_DIM
CHUNKS = 2
FIRST_CHUNKS = 4
MESH = pl.DeviceIdType.MESH

inv_root2 = 0.7071067811865476
inv_root2pi = 0.3989422804014327
norm_eps = 1e-06
VMEM_LIMIT = 63 << 20


def dense(left, right):
    return jnp.dot(left, right, preferred_element_type=jnp.float32)


def dense_tn(left, right):
    return lax.dot_general(
        left, right, (((0,), (0,)), ((), ())), preferred_element_type=jnp.float32
    )


def dense_nt(left, right):
    return lax.dot_general(
        left, right, (((1,), (1,)), ((), ())), preferred_element_type=jnp.float32
    )


def mean_last(values):
    return jnp.mean(values, axis=-1, keepdims=True)


def norm_parts(resid):
    center = resid - mean_last(resid)
    inverse = lax.rsqrt(mean_last(center * center) + norm_eps)
    return center * inverse, inverse


def norm_back(normed, inverse, gain, upstream):
    scaled = upstream * gain
    return inverse * (scaled - mean_last(scaled) - normed * mean_last(scaled * normed))


def span(start, size):
    return pl.ds(pl.multiple_of(start, size), size)


class Place:
    def __init__(self):
        self.dp_size, self.tensor_size = lax.axis_size("dp"), lax.axis_size("tensor")
        self.quads, self.half = self.dp_size // 2, self.tensor_size // 2
        dp, tensor = lax.axis_index("dp"), lax.axis_index("tensor")
        self.q, self.c = lax.div(dp, 2), lax.rem(dp, 2)
        self.h, self.l = lax.div(tensor, self.half), lax.rem(tensor, self.half)
        self.rank = self.c * self.half + self.l
        self.column = self.c * self.tensor_size + tensor
        self.stays = self.c == self.h

    def at(self, q, c, h, l):
        return (2 * q + c, h * self.half + l)

    def beside(self):
        return self.at(self.q, 1 - self.c, self.h, self.l)

    def swapped(self):
        return self.at(self.q, self.h, self.c, self.l)

    def along(self, j):
        return lax.rem(self.l + j, self.half)

    def across(self, j):
        return lax.rem(self.q + j, self.quads)

    def quad_pair(self):
        x, y = lax.rem(self.q, 2), lax.div(self.q, 2)
        return 2 * y + 1 - x, 2 * (1 - y) + x, 2 * (1 - y) + 1 - x

    def in_quad(self, q):
        return self.at(q, self.c, self.h, self.l)

    def column_peer(self, j):
        spot = lax.rem(self.column + j, 2 * self.tensor_size)
        c, tensor = lax.div(spot, self.tensor_size), lax.rem(spot, self.tensor_size)
        return spot, (2 * self.q + c, tensor)

    def greet(self):
        barrier = pltpu.get_barrier_semaphore()
        for j in range(1, 2 * self.tensor_size):
            pl.semaphore_signal(barrier, inc=1, device_id=self.column_peer(j)[1], device_id_type=MESH)
        for j in range(1, self.quads):
            other = self.at(self.across(j), self.c, self.h, self.l)
            pl.semaphore_signal(barrier, inc=1, device_id=other, device_id_type=MESH)
        pl.semaphore_wait(barrier, 2 * self.tensor_size + self.quads - 2)


class Mover:
    def __init__(self, place):
        self.place, self.open = place, []

    def send(self, source, target, send_sem, recv_sem, device, only=None):
        copy = pltpu.make_async_remote_copy(
            src_ref=source,
            dst_ref=target,
            send_sem=send_sem,
            recv_sem=recv_sem,
            device_id=device,
            device_id_type=MESH,
        )
        if only is None:
            copy.start()
        else:
            pl.when(only)(copy.start)
        self.open.append((copy, only))

    def keep_or_send(self, source, target, send_sem, recv_sem, device, is_self):
        self.send(source, target, send_sem, recv_sem, device, jnp.logical_not(is_self))
        pl.when(is_self)(pltpu.make_async_copy(source, target, recv_sem).start)

    def landed(self, target, recv_sem):
        pltpu.make_async_copy(target, target, recv_sem).wait()

    def since(self, mark):
        taken, self.open = self.open[mark:], self.open[:mark]
        return taken

    def finish(self, sends):
        for copy, only in sends:
            if only is None:
                copy.wait_send()
            else:
                pl.when(only)(copy.wait_send)

    def close(self):
        self.finish(self.since(0))


def rows_out(mv, buf, block_rows, chunk, send_sem, recv_sem):
    pc = mv.place
    size = block_rows // recv_sem.shape[1]
    part = buf.at[span(pc.rank * block_rows + chunk * size, size)]
    for j in range(1, pc.half):
        other = pc.at(pc.q, pc.c, pc.h, pc.along(j))
        mv.send(part, part, send_sem.at[chunk, j], recv_sem.at[pc.rank, chunk], other)
    mv.send(part, part, send_sem.at[chunk, 0], recv_sem.at[pc.rank, chunk], pc.beside())


def rows_pass(mv, buf, block_rows, j, chunk, pass_sem, recv_sem):
    pc = mv.place
    size = block_rows // recv_sem.shape[1]
    block = pc.c * pc.half + pc.along(j)
    part = buf.at[span(block * block_rows + chunk * size, size)]
    mv.landed(part, recv_sem.at[block, chunk])
    mv.send(part, part, pass_sem.at[chunk, j], recv_sem.at[block, chunk], pc.beside())


def rows_in(mv, buf, block_rows, j, chunk, recv_sem):
    pc = mv.place
    size = block_rows // recv_sem.shape[1]
    block = (1 - pc.c) * pc.half + pc.along(j)
    part = buf.at[span(block * block_rows + chunk * size, size)]
    mv.landed(part, recv_sem.at[block, chunk])


def weights_pass(mv, size, dest, cols, seg, recv_sem, pass_sem, far_sem):
    pc = mv.place
    for c in range(2):
        mv.landed(dest.at[span((2 * pc.q + c) * size, size), cols], recv_sem.at[seg, c])
    both = dest.at[span(2 * pc.q * size, 2 * size), cols]
    if pc.quads == 4:
        for j, quad in enumerate(pc.quad_pair()[:2]):
            mv.send(both, both, pass_sem.at[seg, j], far_sem.at[seg, j], pc.in_quad(quad))
        return
    for j in range(1, pc.quads):
        other = pc.in_quad(pc.across(j))
        mv.send(both, both, pass_sem.at[seg, j - 1], far_sem.at[seg, pc.quads - j - 1], other)


def weights_relay(mv, size, dest, cols, seg, pass_sem, far_sem):
    pc = mv.place
    if pc.quads != 4:
        return
    quads = pc.quad_pair()
    for j in range(2):
        mv.landed(dest.at[span(2 * quads[j] * size, 2 * size), cols], far_sem.at[seg, j])
        part = dest.at[span((2 * quads[j] + j) * size, size), cols]
        mv.send(part, part, pass_sem.at[seg, 2 + j], far_sem.at[seg, 2 + j], pc.in_quad(quads[1 - j]))


def weights_in(mv, size, dest, cols, seg, far_sem):
    pc = mv.place
    if pc.quads == 4:
        for j in range(2):
            part = dest.at[span((2 * pc.quad_pair()[2] + j) * size, size), cols]
            mv.landed(part, far_sem.at[seg, 2 + j])
        return
    for j in range(1, pc.quads):
        part = dest.at[span(2 * pc.across(j) * size, 2 * size), cols]
        mv.landed(part, far_sem.at[seg, j - 1])


def over_tiles(width, body, most=256):
    tile = min(most, width)

    def step(i, carry):
        body(span(i * tile, tile))
        return carry

    lax.fori_loop(0, width // tile, step, 0)


def reduce_rows(mv, s, sems, own, width, partial):
    pc = mv.place
    size = own // CHUNKS
    send_a, recv_a, send_z, recv_z = sems
    order = list(range(1, pc.half)) + [0]
    mark = len(mv.open)
    for j in order:
        block = (1 - pc.c) * pc.half + pc.along(j)

        def give(tile, j=j, block=block):
            s.core_out[j, :, tile] = partial(block, tile).astype(jnp.bfloat16)

        over_tiles(width, give)
        mv.send(s.core_out.at[j], s.core_in.at[j], send_a.at[j], recv_a.at[j], pc.beside())
    for j in order:
        block = pc.c * pc.half + pc.along(j)
        mv.landed(s.core_in.at[j], recv_a.at[j])
        if j:

            def add(tile, j=j, block=block):
                total = partial(block, tile) + s.core_in[j, :, tile].astype(jnp.float32)
                s.chip_out[j - 1, :, tile] = total.astype(jnp.bfloat16)

            over_tiles(width, add)
            other = pc.at(pc.q, pc.c, pc.h, pc.along(j))
            for k in range(CHUNKS):
                rows = pl.ds(k * size, size)
                mv.send(
                    s.chip_out.at[j - 1, rows],
                    s.chip_in.at[pc.half - j - 1, rows],
                    send_z.at[j, k],
                    recv_z.at[pc.half - j, k],
                    other,
                )
        else:

            def hold(tile, block=block):
                total = partial(block, tile) + s.core_in[0, :, tile].astype(jnp.float32)
                s.held[:, tile] = total

            over_tiles(width, hold)
    return mv.since(mark)


def reduced_chunk(mv, s, sems, own, k):
    pc = mv.place
    size = own // CHUNKS
    rows = pl.ds(k * size, size)
    total = s.held[rows, :]
    for j in range(1, pc.half):
        mv.landed(s.chip_in.at[j - 1, rows], sems[3].at[j, k])
        total = total + s.chip_in[j - 1, rows, :].astype(jnp.float32)
    return total


def in_order(mv, buf, own, pass_sem, recv_sem, work, between=None):
    pc = mv.place
    for j in range(pc.half):
        if j:
            for k in range(recv_sem.shape[1]):
                rows_pass(mv, buf, own, j, k, pass_sem, recv_sem)
        work(pc.c * pc.half + pc.along(j))
        for k in range(recv_sem.shape[1]):
            rows_in(mv, buf, own, j, k, recv_sem)
        work((1 - pc.c) * pc.half + pc.along(j))
        if j == 0 and between is not None:
            between()


def to_group(mv, own, source, target, send_sem, recv_sem):
    pc = mv.place
    size = pc.tensor_size
    for j in range(1, size):
        rank = lax.rem(pc.rank + j, size)
        other = pc.at(pc.q, lax.div(rank, pc.half), pc.h, lax.rem(rank, pc.half))
        mv.send(source(rank), target, send_sem.at[j], recv_sem.at[size - j], other)


def grad_out(mv, s, shard, start, width, left, right, seg):
    pc = mv.place

    def rows_of(quad):
        return span(2 * shard * quad, 2 * shard)

    def fill_rows(rows):
        def fill(tile):
            tile_at = pl.ds(pl.multiple_of(start + tile.start, tile.size), tile.size)
            s.grads[rows, tile_at] = dense_tn(left(rows), right(tile)).astype(jnp.bfloat16)

        over_tiles(width, fill)

    if pc.quads == 4:
        quads = pc.quad_pair()
        fill_rows(rows_of(quads[2]))
        for way in range(2):
            cols = pl.ds(start + way * (width // 2), width // 2)
            fill_rows(rows_of(quads[way]))
            for slot, quad in ((1, quads[2]), (0, quads[way])):
                mv.send(
                    s.grads.at[rows_of(quad), cols],
                    s.grads_in.at[slot, :, cols],
                    s.grad_send.at[seg, 2 * way + slot],
                    s.grad_recv.at[seg, 2 * way + slot],
                    pc.in_quad(quads[way]),
                )
        fill_rows(rows_of(pc.q))
        return
    cols = pl.ds(start, width)
    for at in range(0, s.grads.shape[0], 128):
        fill_rows(pl.ds(at, 128))
    for j in range(1, pc.quads):
        quad = pc.across(j)
        mv.send(
            s.grads.at[rows_of(quad), cols],
            s.grads_in.at[pc.quads - j - 1, :, cols],
            s.grad_send.at[seg, j],
            s.grad_recv.at[seg, pc.quads - j],
            pc.in_quad(quad),
        )


def grad_pass(mv, s, shard, start, width, seg):
    pc = mv.place
    if pc.quads != 4:
        return
    quads = pc.quad_pair()
    for way in range(2):
        at = start + way * (width // 2)
        cols = pl.ds(at, width // 2)
        other = quads[1 - way]
        rows = span(2 * shard * other, 2 * shard)
        mv.landed(s.grads_in.at[1, :, cols], s.grad_recv.at[seg, 2 * way + 1])

        def add(tile, at=at, rows=rows):
            tile_at = pl.ds(pl.multiple_of(at + tile.start, 128), tile.size)
            value = s.grads[rows, tile_at].astype(jnp.float32) + s.grads_in[1, :, tile_at].astype(jnp.float32)
            s.grads[rows, tile_at] = value.astype(jnp.bfloat16)

        over_tiles(width // 2, add, 128)
        mv.send(
            s.grads.at[rows, cols],
            s.grads_in.at[2, :, cols],
            s.grad_send.at[seg, 4 + way],
            s.grad_recv.at[seg, 4 + way],
            pc.in_quad(other),
        )


def grad_sum(mv, s, shard, start, width, seg, result):
    pc = mv.place
    cols = pl.ds(start, width)
    if pc.quads == 4:
        for way in range(2):
            part = pl.ds(start + way * (width // 2), width // 2)
            mv.landed(s.grads_in.at[0, :, part], s.grad_recv.at[seg, 2 * way])
            mv.landed(s.grads_in.at[2, :, part], s.grad_recv.at[seg, 4 + way])
        slots = (0, 2)
    else:
        for j in range(1, pc.quads):
            mv.landed(s.grads_in.at[j - 1, :, cols], s.grad_recv.at[seg, j])
        slots = tuple(range(pc.quads - 1))

    def total(tile):
        tile_at = pl.ds(pl.multiple_of(start + tile.start, tile.size), tile.size)
        value = s.grads[span(2 * shard * pc.q, 2 * shard), tile_at].astype(jnp.float32)
        for slot in slots:
            value = value + s.grads_in[slot, :, tile_at].astype(jnp.float32)
        s.grads_out[:, tile_at] = value.astype(jnp.bfloat16)

    over_tiles(width, total)
    for core in range(2):
        mv.keep_or_send(
            s.grads_out.at[pl.ds(core * shard, shard), cols],
            result.at[pc.h, :, cols],
            s.owner_send.at[seg, core],
            s.owner_recv.at[seg, pc.h],
            pc.at(pc.q, core, pc.c, pc.l),
            jnp.logical_and(pc.stays, pc.c == core),
        )


def layer_kernel(names, *refs):
    by_name = dict(zip(names, refs))
    s = types.SimpleNamespace(**by_name)
    sems_ra = (s.ra_send_a, s.ra_recv_a, s.ra_send_z, s.ra_recv_z)
    sems_rb = (s.rb_send_a, s.rb_recv_a, s.rb_send_z, s.rb_recv_z)
    sems_rc = (s.rc_send_a, s.rc_recv_a, s.rc_send_z, s.rc_recv_z)
    pc = Place()
    mv = Mover(pc)
    seq, wide = s.seq, s.wide
    own = s.x.shape[0]
    size = own // CHUNKS
    total_rows, width = seq.shape
    heads = wide.shape[1]
    hidden = s.inner.shape[1]
    shard = s.key_part.shape[0]
    group = pc.tensor_size
    pairs = heads // PAIR
    mine = span(pc.rank * own, own)
    vec, sums = s.vec, s.sums
    f32 = jnp.float32
    inner, hid_cols, head_part = s.inner, pl.ds(0, hidden), pl.ds(0, heads)
    scale = HEAD_DIM ** (-0.5)

    def block_rows(block):
        return span(block * own, own)

    def own_chunk(k):
        return span(pc.rank * own + k * size, size)

    def stack(buf, part):
        return buf.at[pl.ds(part * width, width)]

    def stacked(part, tile):
        return pl.ds(pl.multiple_of(part * width + tile.start, tile.size), tile.size)

    new_rank = pc.h * pc.half + pc.l
    new_out = s.out_all.at[span(new_rank * width, width)]
    my_out = s.out_all.at[span(pc.rank * width, width)]
    parts = (
        (s.out_turned, new_out, my_out, pl.ds(0, heads)),
        (s.inner_part, stack(inner, 0), stack(inner, 0), hid_cols),
        (s.outer_turned, stack(inner, 1), stack(inner, 1), hid_cols),
        (s.query_part, stack(wide, 0), stack(wide, 0), head_part),
        (s.key_part, stack(wide, 1), stack(wide, 1), head_part),
        (s.value_part, stack(wide, 2), stack(wide, 2), head_part),
    )
    attn_parts = (3, 4, 5)

    def start_weight(seg):
        source, target, _, cols = parts[seg]
        place = span((2 * pc.q + pc.c) * shard, shard)
        for half in range(2):
            mv.keep_or_send(
                source,
                target.at[place, cols],
                s.w_send.at[seg, half],
                s.w_recv.at[seg, pc.c],
                pc.at(pc.q, pc.h, half, pc.l),
                jnp.logical_and(pc.stays, pc.h == half),
            )

    def pass_weight(seg):
        weights_pass(mv, shard, parts[seg][2], parts[seg][3], seg, s.w_recv, s.w_pass, s.w_far)

    def relay_weight(seg):
        weights_relay(mv, shard, parts[seg][2], parts[seg][3], seg, s.w_pass, s.w_far)

    def end_weight(seg):
        weights_in(mv, shard, parts[seg][2], parts[seg][3], seg, s.w_far)

    pc.greet()
    column_size = 2 * group
    first = own // FIRST_CHUNKS
    every = s.every
    spot = (2 * pc.q + pc.c) * group + pc.h * pc.half + pc.l
    keep = pltpu.make_async_copy(s.vectors, every.at[spot], s.v_recv.at[0])
    keep.start()
    for j in range(1, column_size):
        mv.send(s.vectors, every.at[spot], s.v_send.at[j], s.v_recv.at[column_size - j], pc.column_peer(j)[1])
    for seg in attn_parts:
        start_weight(seg)
    s.out_turned[...] = jnp.transpose(s.out_part[...])
    s.outer_turned[...] = jnp.transpose(s.outer_part[...])
    sums[...] = jnp.zeros_like(sums)
    keep.wait()
    for j in range(1, column_size):
        mv.landed(every.at[spot], s.v_recv.at[j])
    column = every.at[span(2 * pc.q * group, column_size)]
    for j in range(1, pc.quads):
        mv.send(column, column, s.v_pass.at[j], s.v_far.at[pc.quads - j], pc.in_quad(pc.across(j)))
    for seg in attn_parts:
        pass_weight(seg)
    for k in range(FIRST_CHUNKS):
        mv.keep_or_send(
            s.x.at[pl.ds(k * first, first)],
            seq.at[span(new_rank * own + k * first, first)],
            s.swap_send.at[k],
            s.swap_recv.at[k],
            pc.swapped(),
            pc.stays,
        )
    start_weight(0)
    for j in range(1, pc.quads):
        mv.landed(column, s.v_far.at[j])
    piece = width // (pc.dp_size * group)
    vec[...] = jnp.zeros_like(vec)
    for i in range(pc.dp_size * group):
        vec[0:6, i * piece : (i + 1) * piece] = every[i, 0:6, 0:piece]
    qv_piece, in_piece = heads // pc.dp_size, hidden // pc.dp_size
    for i in range(pc.dp_size):
        held = every[i * group + pc.rank]
        for part in range(2):
            vec[6:7, part * heads + i * qv_piece : part * heads + (i + 1) * qv_piece] = (
                held[6:7, part * qv_piece : (part + 1) * qv_piece]
            )
        vec[7:8, i * in_piece : (i + 1) * in_piece] = held[7:8, 0:in_piece]
    length = every[(2 * pc.q + pc.h) * group][6:7, 127:128]
    for k in range(FIRST_CHUNKS):
        mv.landed(seq.at[span(pc.rank * own + k * first, first)], s.swap_recv.at[k])
        rows_out(mv, seq, own, k, s.row_send, s.row_recv)
        if k == FIRST_CHUNKS - 2:
            for seg in attn_parts:
                relay_weight(seg)
    pass_weight(0)
    start_weight(1)
    for seg in attn_parts:
        end_weight(seg)
    relay_weight(0)

    qkv = s.qkv

    def project(block):
        rows = block_rows(block)
        query = (dense(seq[rows, :], wide[0:width, :]) + vec[6:7, 0:heads]).astype(jnp.bfloat16)
        qkv[rows, 0:heads] = (query.astype(f32) * scale).astype(jnp.bfloat16)
        qkv[rows, heads : 2 * heads] = dense(seq[rows, :], wide[width : 2 * width, :]).astype(jnp.bfloat16)
        value = dense(seq[rows, :], wide[2 * width : 3 * width, :]) + vec[6:7, heads : 2 * heads]
        qkv[rows, 2 * heads : 3 * heads] = value.astype(jnp.bfloat16)

    in_order(mv, seq, own, s.row_pass, s.row_recv, project)
    end_weight(0)
    for k in range(CHUNKS):
        rows_out(mv, s.out_all, width, k, s.out_send, s.out_recv)

    step_rows = min(256, total_rows)
    spot = lax.broadcasted_iota(jnp.int32, (1, total_rows), 1).astype(f32)
    bias = jnp.where(spot < length, 0.0, -jnp.inf).astype(f32)

    def head_cols(pair, head, part):
        start = part * heads + pair * PAIR + head * HEAD_DIM
        return slice(start, start + HEAD_DIM)

    for pair in range(pairs):

        def attend(i, carry, pair=pair):
            rows = span(i * step_rows, step_rows)
            found = []
            for head in range(2):
                scores = dense_nt(qkv[rows, head_cols(pair, head, 0)], qkv[:, head_cols(pair, head, 1)]) + bias
                top = jnp.max(scores, axis=-1, keepdims=True)
                grown = jnp.exp(scores - top)
                total = jnp.sum(grown, axis=-1, keepdims=True)
                probs = (grown * (1.0 / total)).astype(jnp.bfloat16)
                lane = 2 * pair + head
                s.log_total[rows, lane : lane + 1] = top + jnp.log(total)
                found.append(dense(probs, qkv[:, head_cols(pair, head, 2)]))
            s.ctx[rows, pair * PAIR : (pair + 1) * PAIR] = jnp.concatenate(found, axis=1).astype(jnp.bfloat16)
            return carry

        lax.fori_loop(0, total_rows // step_rows, attend, 0)
        place = span(pc.rank * heads + pair * PAIR, PAIR)
        pair_cols = pl.ds(pair * PAIR, PAIR)
        to_group(
            mv, own,
            lambda rank, cols=pair_cols: s.ctx.at[span(rank * own, own), cols],
            s.own_ctx.at[:, place],
            s.ctx_send.at[pair], s.ctx_recv.at[pair],
        )
        s.own_ctx[:, place] = s.ctx[mine, pair_cols]
        if pair == 0:
            for j in range(1, pc.half):
                for k in range(CHUNKS):
                    rows_pass(mv, s.out_all, width, j, k, s.out_pass, s.out_recv)
            pass_weight(1)
            start_weight(2)
    mv.keep_or_send(s.cot, s.cot_in, s.cot_send.at[0], s.cot_recv.at[0], pc.swapped(), pc.stays)
    for pair in range(pairs):
        for j in range(1, group):
            mv.landed(s.own_ctx.at[:, pl.ds(0, PAIR)], s.ctx_recv.at[pair, j])
    relay_weight(1)
    pass_weight(2)
    for j in range(pc.half):
        for k in range(CHUNKS):
            rows_in(mv, s.out_all, width, j, k, s.out_recv)

    for k in range(CHUNKS):
        rows = pl.ds(k * size, size)
        total = seq[own_chunk(k), :].astype(f32) + vec[0:1, :]
        for t in range(group):
            total = total + dense_nt(
                s.own_ctx[rows, t * heads : (t + 1) * heads], s.out_all[t * width : (t + 1) * width, :]
            )
        s.resid[rows, :] = total
        normed, _ = norm_parts(total)
        middle = normed * vec[1:2, :] + vec[2:3, :]
        s.middle[rows, :] = middle
        s.mid_rows[own_chunk(k), :] = middle.astype(jnp.bfloat16)
        rows_out(mv, s.mid_rows, own, k, s.mid_send, s.mid_recv)

    end_weight(1)

    def expand(block):
        rows = block_rows(block)

        def one(tile):
            pre = dense(s.mid_rows[rows, :], inner[0:width, tile]) + vec[7:8, tile]
            cdf = 0.5 * (1.0 + lax.erf(pre * inv_root2))
            s.hid[rows, tile] = (pre * cdf).astype(jnp.bfloat16)
            s.slope[rows, tile] = cdf + pre * inv_root2pi * jnp.exp(-0.5 * pre * pre)

        over_tiles(hidden, one)

    in_order(mv, s.mid_rows, own, s.mid_pass, s.mid_recv, expand, lambda: relay_weight(2))
    end_weight(2)
    sent_ra = reduce_rows(
        mv, s, sems_ra, own, width,
        lambda block, tile: dense_nt(s.hid[block_rows(block), :], inner[stacked(1, tile), :]),
    )
    mv.landed(s.cot_in, s.cot_recv.at[0])
    for k in range(CHUNKS):
        rows = pl.ds(k * size, size)
        total = s.middle[rows, :] + reduced_chunk(mv, s, sems_ra, own, k) + vec[3:4, :]
        normed, inverse = norm_parts(total)
        up = s.cot_in[rows, :].astype(f32)
        d_resid = norm_back(normed, inverse, vec[4:5, :], up)
        s.d_resid[rows, :] = d_resid
        s.ffn_rows[own_chunk(k), :] = d_resid.astype(jnp.bfloat16)
        rows_out(mv, s.ffn_rows, own, k, s.ffn_send, s.ffn_recv)
        sums[3:4, :] += jnp.sum(d_resid, axis=0, keepdims=True)
        sums[4:5, :] += jnp.sum(up * normed, axis=0, keepdims=True)
        sums[5:6, :] += jnp.sum(up, axis=0, keepdims=True)
        s.out_stage[rows, :] = (normed * vec[4:5, :] + vec[5:6, :]).astype(jnp.bfloat16)

    mv.finish(sent_ra)

    def shrink(block):
        rows = block_rows(block)

        def one(tile):
            d_pre = dense(s.ffn_rows[rows, :], inner[width : 2 * width, tile]) * s.slope[rows, tile]
            sums[7:8, tile] += jnp.sum(d_pre, axis=0, keepdims=True)
            s.d_pre[rows, tile] = d_pre.astype(jnp.bfloat16)

        over_tiles(hidden, one)

    in_order(mv, s.ffn_rows, own, s.ffn_pass, s.ffn_recv, shrink)
    sent_rb = reduce_rows(
        mv, s, sems_rb, own, width,
        lambda block, tile: dense_nt(s.d_pre[block_rows(block), :], inner[tile, :]),
    )
    for k in range(CHUNKS):
        rows = pl.ds(k * size, size)
        mv.keep_or_send(
            s.out_stage.at[rows], s.block_out.at[rows],
            s.bo_send.at[k], s.bo_recv.at[k], pc.swapped(), pc.stays,
        )
    at_out, at_in, at_outer = 3 * heads, 4 * heads, 4 * heads + hidden
    grad_out(
        mv, s, shard, at_outer, hidden,
        lambda rows: s.ffn_rows[:, rows], lambda tile: s.hid[:, tile], 0,
    )
    grad_out(
        mv, s, shard, at_in, hidden,
        lambda rows: s.mid_rows[:, rows], lambda tile: s.d_pre[:, tile], 1,
    )
    for k in range(CHUNKS):
        rows = pl.ds(k * size, size)
        up = reduced_chunk(mv, s, sems_rb, own, k) + s.d_resid[rows, :]
        normed, inverse = norm_parts(s.resid[rows, :])
        d_resid = norm_back(normed, inverse, vec[1:2, :], up)
        s.d_resid[rows, :] = d_resid
        s.attn_rows[own_chunk(k), :] = d_resid.astype(jnp.bfloat16)
        sums[0:1, :] += jnp.sum(d_resid, axis=0, keepdims=True)
        sums[1:2, :] += jnp.sum(up * normed, axis=0, keepdims=True)
        sums[2:3, :] += jnp.sum(up, axis=0, keepdims=True)

    mv.finish(sent_rb)

    for t in range(group):
        s.d_ctx_out[t, :, :] = dense(
            s.attn_rows[mine, :], s.out_all[t * width : (t + 1) * width, :]
        ).astype(jnp.bfloat16)
    to_group(
        mv, own,
        lambda rank: s.d_ctx_out.at[rank],
        s.d_ctx.at[mine],
        s.d_ctx_send, s.d_ctx_recv,
    )
    s.d_ctx[mine, :] = s.d_ctx_out[pc.rank, :, :]
    for k in range(CHUNKS):
        rows_out(mv, s.attn_rows, own, k, s.at_send, s.at_recv)
    for j in range(1, group):
        mv.landed(s.d_ctx.at[mine], s.d_ctx_recv.at[j])
    d_qkv = s.d_qkv
    grad_pass(mv, s, shard, at_outer, hidden, 0)
    for pair in range(pairs):
        s.key_sum[...] = jnp.zeros_like(s.key_sum)
        s.value_sum[...] = jnp.zeros_like(s.value_sum)

        def attend_back(i, carry, pair=pair):
            rows = span(i * step_rows, step_rows)
            found = []
            for head in range(2):
                cols = slice(head * HEAD_DIM, (head + 1) * HEAD_DIM)
                lane = 2 * pair + head
                query, key = qkv[rows, head_cols(pair, head, 0)], qkv[:, head_cols(pair, head, 1)]
                grad = s.d_ctx[rows, head_cols(pair, head, 0)]
                scores = dense_nt(query, key) + bias
                probs = jnp.exp(scores - s.log_total[rows, lane : lane + 1])
                d_probs = dense_nt(grad, qkv[:, head_cols(pair, head, 2)])
                within = jnp.sum(probs * d_probs, axis=-1, keepdims=True)
                d_scores = (probs * (d_probs - within)).astype(jnp.bfloat16)
                found.append(dense(d_scores, key) * scale)
                s.value_sum[cols, :] += dense_tn(grad, probs.astype(jnp.bfloat16))
                s.key_sum[cols, :] += dense_tn(query, d_scores)
            d_query = jnp.concatenate(found, axis=1)
            d_qkv[rows, pair * PAIR : (pair + 1) * PAIR] = d_query.astype(jnp.bfloat16)
            sums[6:7, pair * PAIR : (pair + 1) * PAIR] += jnp.sum(d_query, axis=0, keepdims=True)
            return carry

        lax.fori_loop(0, total_rows // step_rows, attend_back, 0)
        at_key = slice(heads + pair * PAIR, heads + (pair + 1) * PAIR)
        at_value = slice(2 * heads + pair * PAIR, 2 * heads + (pair + 1) * PAIR)
        d_qkv[:, at_key] = jnp.transpose(s.key_sum[...]).astype(jnp.bfloat16)
        d_value = jnp.transpose(s.value_sum[...])
        d_qkv[:, at_value] = d_value.astype(jnp.bfloat16)
        sums[6:7, at_key] = jnp.sum(d_value, axis=0, keepdims=True)
        if pair == 0:
            grad_sum(mv, s, shard, at_outer, hidden, 0, s.weight_grads)
            grad_pass(mv, s, shard, at_in, hidden, 1)
            for j in range(1, pc.half):
                for k in range(CHUNKS):
                    rows_pass(mv, s.attn_rows, own, j, k, s.at_pass, s.at_recv)
            for j in range(pc.half):
                for k in range(CHUNKS):
                    rows_in(mv, s.attn_rows, own, j, k, s.at_recv)
            grad_out(
                mv, s, shard, at_out, heads,
                lambda rows: s.attn_rows[:, rows], lambda tile: s.ctx[:, tile], 2,
            )
    slots = s.sum_slots
    slots[pc.column] = sums[...]
    for j in range(1, 2 * group):
        mv.send(
            sums, slots.at[pc.column],
            s.sum_send.at[j], s.sum_recv.at[2 * group - j], pc.column_peer(j)[1],
        )
    grad_out(
        mv, s, shard, 0, 3 * heads,
        lambda rows: seq[:, rows], lambda tile: d_qkv[:, tile], 3,
    )
    sent_rc = reduce_rows(
        mv, s, sems_rc, own, width,
        lambda block, tile: sum(
            dense_nt(d_qkv[block_rows(block), part * heads : (part + 1) * heads], wide[stacked(part, tile), :])
            for part in range(3)
        ),
    )
    grad_sum(mv, s, shard, at_in, hidden, 1, s.weight_grads)
    grad_pass(mv, s, shard, at_out, heads, 2)
    grad_sum(mv, s, shard, at_out, heads, 2, s.weight_grads)
    for k in range(CHUNKS):
        if k == CHUNKS // 2:
            grad_pass(mv, s, shard, 0, 3 * heads, 3)
        rows = pl.ds(k * size, size)
        s.ig_stage[rows, :] = (reduced_chunk(mv, s, sems_rc, own, k) + s.d_resid[rows, :]).astype(jnp.bfloat16)
        mv.keep_or_send(
            s.ig_stage.at[rows], s.input_grad.at[rows],
            s.ig_send.at[k], s.ig_recv.at[k], pc.swapped(), pc.stays,
        )
    mv.finish(sent_rc)
    for j in range(1, 2 * group):
        mv.landed(slots.at[0], s.sum_recv.at[j])
    whole = slots[0]
    for j in range(1, 2 * group):
        whole = whole + slots[j]
    chosen = pc.h * group + pc.l
    biases = slots[chosen] + slots[chosen + pc.half]
    row = lax.broadcasted_iota(jnp.int32, whole.shape, 0)
    summed = jnp.where(row < 6, whole, biases)
    s.sum_stage[...] = summed
    for j in range(1, pc.quads):
        other = pc.at(pc.across(j), pc.c, pc.h, pc.l)
        mv.send(s.sum_stage, s.sum_far.at[pc.quads - j - 1], s.far_send.at[j], s.far_recv.at[pc.quads - j], other)
    for j in range(1, pc.quads):
        mv.landed(s.sum_stage, s.far_recv.at[j])
        summed = summed + s.sum_far[j - 1]
    s.vec_grads[...] = summed
    grad_sum(mv, s, shard, 0, 3 * heads, 3, s.weight_grads)
    for k in range(CHUNKS):
        rows = pl.ds(k * size, size)
        mv.landed(s.block_out.at[rows], s.bo_recv.at[k])
        mv.landed(s.input_grad.at[rows], s.ig_recv.at[k])
    for seg, (start, count) in enumerate(
        ((at_outer, hidden), (at_in, hidden), (at_out, heads), (0, 3 * heads))
    ):
        for h in range(2):
            mv.landed(s.weight_grads.at[h, :, pl.ds(start, count)], s.owner_recv.at[seg, h])
    mv.close()


def run_layer(x, query_part, key_part, value_part, out_part, inner_part, outer_part, vectors, cot):
    dp_size, tensor_size = lax.axis_size("dp"), lax.axis_size("tensor")
    quads, half = dp_size // 2, tensor_size // 2
    own, width = x.shape
    rows = own * tensor_size
    shard, heads = query_part.shape
    hidden = inner_part.shape[1]
    pairs = heads // PAIR
    every = 4 * heads + 2 * hidden
    bf16, f32 = jnp.bfloat16, jnp.float32
    ins = dict(
        x=x, query_part=query_part, key_part=key_part, value_part=value_part, inner_part=inner_part,
        vectors=vectors, cot=cot, out_part=out_part, outer_part=outer_part,
    )
    outs = dict(
        block_out=((own, width), bf16),
        input_grad=((own, width), bf16),
        weight_grads=((2, shard, every), bf16),
        vec_grads=((8, width), f32),
    )
    buffers = dict(
        seq=((rows, width), bf16),
        wide=((3 * width, heads), bf16),
        vec=((8, width), f32),
        every=((dp_size * tensor_size,) + vectors.shape, f32),
        out_turned=((shard, heads), bf16),
        outer_turned=((shard, hidden), bf16),
        inner=((2 * width, hidden), bf16),
        out_all=((tensor_size * width, heads), bf16),
        qkv=((rows, 3 * heads), bf16),
        log_total=((rows, 128), f32),
        ctx=((rows, heads), bf16),
        own_ctx=((own, width), bf16),
        resid=((own, width), f32),
        middle=((own, width), f32),
        d_resid=((own, width), f32),
        held=((own, width), f32),
        mid_rows=((rows, width), bf16),
        slope=((rows, hidden), f32),
        hid=((rows, hidden), bf16),
        ffn_rows=((rows, width), bf16),
        d_pre=((rows, hidden), bf16),
        attn_rows=((rows, width), bf16),
        d_ctx_out=((tensor_size, own, heads), bf16),
        d_ctx=((rows, heads), bf16),
        d_qkv=((rows, 3 * heads), bf16),
        key_sum=((PAIR, rows), f32),
        value_sum=((PAIR, rows), f32),
        core_out=((half, own, width), bf16),
        core_in=((half, own, width), bf16),
        chip_out=((half - 1, own, width), bf16),
        chip_in=((half - 1, own, width), bf16),
        grads=((width, every), bf16),
        grads_in=((quads - 1, 2 * shard, every), bf16),
        grads_out=((2 * shard, every), bf16),
        cot_in=((own, width), bf16),
        out_stage=((own, width), bf16),
        ig_stage=((own, width), bf16),
        sums=((8, width), f32),
        sum_slots=((2 * tensor_size, 8, width), f32),
        sum_stage=((8, width), f32),
        sum_far=((quads - 1, 8, width), f32),
    )
    sems = dict(
        w_send=(6, 2), w_recv=(6, 2), w_pass=(6, quads), w_far=(6, quads),
        swap_send=(FIRST_CHUNKS,), swap_recv=(FIRST_CHUNKS,),
        v_send=(2 * tensor_size,), v_recv=(2 * tensor_size,), v_pass=(quads,), v_far=(quads,),
        cot_send=(1,), cot_recv=(1,),
        ctx_send=(pairs, tensor_size), ctx_recv=(pairs, tensor_size),
        d_ctx_send=(tensor_size,), d_ctx_recv=(tensor_size,),
        bo_send=(CHUNKS,), bo_recv=(CHUNKS,), ig_send=(CHUNKS,), ig_recv=(CHUNKS,),
        grad_send=(4, quads + 2), grad_recv=(4, quads + 2), owner_send=(4, 2), owner_recv=(4, 2),
        sum_send=(2 * tensor_size,), sum_recv=(2 * tensor_size,), far_send=(quads,), far_recv=(quads,),
    )
    for tag in ("row", "out", "mid", "ffn", "at"):
        sems[tag + "_send"] = (CHUNKS, half)
        sems[tag + "_recv"] = (tensor_size, CHUNKS)
        sems[tag + "_pass"] = (CHUNKS, half)
    sems.update(
        row_send=(FIRST_CHUNKS, half), row_recv=(tensor_size, FIRST_CHUNKS), row_pass=(FIRST_CHUNKS, half)
    )
    for tag in ("ra", "rb", "rc"):
        sems[tag + "_send_a"] = (half,)
        sems[tag + "_recv_a"] = (half,)
        sems[tag + "_send_z"] = (half, CHUNKS)
        sems[tag + "_recv_z"] = (half, CHUNKS)
    names = tuple(ins) + tuple(outs) + tuple(buffers) + tuple(sems)
    vmem, anywhere = pl.BlockSpec(memory_space=pltpu.VMEM), pl.BlockSpec(memory_space=pl.ANY)
    return pl.pallas_call(
        functools.partial(layer_kernel, names),
        out_shape=[jax.ShapeDtypeStruct(shape, kind) for shape, kind in outs.values()],
        in_specs=[anywhere] * 7 + [vmem] * 2,
        out_specs=[vmem] * len(outs),
        scratch_shapes=[pltpu.VMEM(shape, kind) for shape, kind in buffers.values()]
        + [pltpu.SemaphoreType.DMA(shape) for shape in sems.values()],
        compiler_params=pltpu.CompilerParams(
            collective_id=0, has_side_effects=True, vmem_limit_bytes=VMEM_LIMIT
        ),
        name="layer",
    )(*ins.values())


def finish_kernel(cuts, block_ref, input_ref, grads_ref, out_block, out_input, *out_grads):
    out_block[...] = block_ref[...]
    out_input[...] = input_ref[...].astype(jnp.float32)
    for i, out in enumerate(out_grads):
        cols = slice(cuts[i], cuts[i + 1])
        total = grads_ref[0, :, cols].astype(jnp.float32) + grads_ref[1, :, cols].astype(jnp.float32)
        out[...] = total if out.shape == total.shape else jnp.transpose(total)


def finish(block_out, input_grad, weight_grads, shapes):
    cuts = [0]
    for shape, turned in shapes:
        cuts.append(cuts[-1] + (shape[0] if turned else shape[1]))
    f32 = jnp.float32
    return pl.pallas_call(
        functools.partial(finish_kernel, cuts),
        out_shape=[
            jax.ShapeDtypeStruct(block_out.shape, block_out.dtype),
            jax.ShapeDtypeStruct(input_grad.shape, f32),
        ]
        + [jax.ShapeDtypeStruct(shape, f32) for shape, _ in shapes],
        compiler_params=pltpu.CompilerParams(vmem_limit_bytes=32 << 20),
        name="finish",
    )(block_out, input_grad, weight_grads)


def per_device(
    block_input,
    lengths,
    query_weight,
    key_weight,
    value_weight,
    query_bias,
    value_bias,
    output_weight,
    output_bias,
    first_gain,
    first_shift,
    inner_weight,
    inner_bias,
    outer_weight,
    outer_bias,
    second_gain,
    second_shift,
    cotangent,
):
    f32 = jnp.float32
    dp_size, tensor_size = lax.axis_size("dp"), lax.axis_size("tensor")
    dp, tensor = lax.axis_index("dp"), lax.axis_index("tensor")

    features = (output_bias, first_gain, first_shift, outer_bias, second_gain, second_shift)
    biases = (query_bias, value_bias, inner_bias)
    def lanes(row):
        return jnp.pad(row, ((0, 0), (0, 128 - row.shape[1])))

    query_bias, value_bias, inner_bias = (bias.astype(f32)[None] for bias in biases)
    mixed = jnp.concatenate([query_bias, value_bias], axis=1)
    length = jnp.broadcast_to(lengths.astype(f32)[None], (1, 128 - mixed.shape[1]))
    vectors = jnp.concatenate(
        [lanes(jnp.stack(features)), jnp.concatenate([mixed, length], axis=1), lanes(inner_bias)]
    )
    block_out, input_grad, weight_grads, vec_grads = run_layer(
        block_input, query_weight, key_weight, value_weight, output_weight, inner_weight, outer_weight,
        vectors, cotangent,
    )

    width = block_input.shape[1]
    heads, hidden = query_weight.shape[1], inner_weight.shape[1]
    block_out, input_grad, *pieces = finish(
        block_out, input_grad, weight_grads,
        (
            (query_weight.shape, False),
            (key_weight.shape, False),
            (value_weight.shape, False),
            (output_weight.shape, True),
            (inner_weight.shape, False),
            (outer_weight.shape, True),
        ),
    )
    piece = width // (dp_size * tensor_size)
    mine = lax.dynamic_slice_in_dim(vec_grads, (dp * tensor_size + tensor) * piece, piece, axis=1)

    def bias_piece(row, start, count):
        size = count // dp_size
        return lax.dynamic_slice(vec_grads, (row, start + dp * size), (1, size))[0]

    return (
        block_out,
        input_grad,
        pieces[0],
        pieces[1],
        pieces[2],
        bias_piece(6, 0, heads),
        bias_piece(6, heads, heads),
        pieces[3],
        mine[0],
        mine[1],
        mine[2],
        pieces[4],
        bias_piece(7, 0, hidden),
        pieces[5],
        mine[3],
        mine[4],
        mine[5],
    )


def solution(mesh):
    return jax.shard_map(
        per_device,
        mesh=mesh,
        in_specs=(
            P(("dp", "tensor"), None),
            P("dp"),
            P("dp", "tensor"),
            P("dp", "tensor"),
            P("dp", "tensor"),
            P(("tensor", "dp")),
            P(("tensor", "dp")),
            P("tensor", "dp"),
            P(("dp", "tensor")),
            P(("dp", "tensor")),
            P(("dp", "tensor")),
            P("dp", "tensor"),
            P(("tensor", "dp")),
            P("tensor", "dp"),
            P(("dp", "tensor")),
            P(("dp", "tensor")),
            P(("dp", "tensor")),
            P(("dp", "tensor"), None),
        ),
        out_specs=(
            P(("dp", "tensor"), None),
            P(("dp", "tensor"), None),
            P("dp", "tensor"),
            P("dp", "tensor"),
            P("dp", "tensor"),
            P(("tensor", "dp")),
            P(("tensor", "dp")),
            P("tensor", "dp"),
            P(("dp", "tensor")),
            P(("dp", "tensor")),
            P(("dp", "tensor")),
            P("dp", "tensor"),
            P(("tensor", "dp")),
            P("tensor", "dp"),
            P(("dp", "tensor")),
            P(("dp", "tensor")),
            P(("dp", "tensor")),
        ),
        check_vma=False,
    )
```

```python
import functools
import types

import jax
import jax.numpy as jnp
from jax import lax
from jax.experimental import pallas as pl
from jax.experimental.pallas import tpu as pltpu
from jax.sharding import PartitionSpec as P

HEAD_DIM = 64
PAIR = 2 * HEAD_DIM
CHUNKS = 2
FIRST_CHUNKS = 4
MESH = pl.DeviceIdType.MESH

inv_root2 = 0.7071067811865476
inv_root2pi = 0.3989422804014327
norm_eps = 1e-06
VMEM_LIMIT = 63 << 20


def dense(left, right):
    return jnp.dot(left, right, preferred_element_type=jnp.float32)


def dense_tn(left, right):
    return lax.dot_general(
        left, right, (((0,), (0,)), ((), ())), preferred_element_type=jnp.float32
    )


def dense_nt(left, right):
    return lax.dot_general(
        left, right, (((1,), (1,)), ((), ())), preferred_element_type=jnp.float32
    )


def mean_last(values):
    return jnp.mean(values, axis=-1, keepdims=True)


def norm_parts(resid):
    center = resid - mean_last(resid)
    inverse = lax.rsqrt(mean_last(center * center) + norm_eps)
    return center * inverse, inverse


def norm_back(normed, inverse, gain, upstream):
    scaled = upstream * gain
    return inverse * (scaled - mean_last(scaled) - normed * mean_last(scaled * normed))


def span(start, size):
    return pl.ds(pl.multiple_of(start, size), size)


class Place:
    def __init__(self):
        self.dp_size, self.tensor_size = lax.axis_size("dp"), lax.axis_size("tensor")
        self.quads, self.half = self.dp_size // 2, self.tensor_size // 2
        dp, tensor = lax.axis_index("dp"), lax.axis_index("tensor")
        self.q, self.c = lax.div(dp, 2), lax.rem(dp, 2)
        self.h, self.l = lax.div(tensor, self.half), lax.rem(tensor, self.half)
        self.rank = self.c * self.half + self.l
        self.column = self.c * self.tensor_size + tensor
        self.stays = self.c == self.h

    def at(self, q, c, h, l):
        return (2 * q + c, h * self.half + l)

    def beside(self):
        return self.at(self.q, 1 - self.c, self.h, self.l)

    def swapped(self):
        return self.at(self.q, self.h, self.c, self.l)

    def along(self, j):
        return lax.rem(self.l + j, self.half)

    def across(self, j):
        return lax.rem(self.q + j, self.quads)

    def quad_pair(self):
        x, y = lax.rem(self.q, 2), lax.div(self.q, 2)
        return 2 * y + 1 - x, 2 * (1 - y) + x, 2 * (1 - y) + 1 - x

    def in_quad(self, q):
        return self.at(q, self.c, self.h, self.l)

    def column_peer(self, j):
        spot = lax.rem(self.column + j, 2 * self.tensor_size)
        c, tensor = lax.div(spot, self.tensor_size), lax.rem(spot, self.tensor_size)
        return spot, (2 * self.q + c, tensor)

    def greet(self):
        barrier = pltpu.get_barrier_semaphore()
        for j in range(1, 2 * self.tensor_size):
            pl.semaphore_signal(barrier, inc=1, device_id=self.column_peer(j)[1], device_id_type=MESH)
        for j in range(1, self.quads):
            other = self.at(self.across(j), self.c, self.h, self.l)
            pl.semaphore_signal(barrier, inc=1, device_id=other, device_id_type=MESH)
        pl.semaphore_wait(barrier, 2 * self.tensor_size + self.quads - 2)


class Mover:
    def __init__(self, place):
        self.place, self.open = place, []

    def send(self, source, target, send_sem, recv_sem, device, only=None):
        copy = pltpu.make_async_remote_copy(
            src_ref=source,
            dst_ref=target,
            send_sem=send_sem,
            recv_sem=recv_sem,
            device_id=device,
            device_id_type=MESH,
        )
        if only is None:
            copy.start()
        else:
            pl.when(only)(copy.start)
        self.open.append((copy, only))

    def keep_or_send(self, source, target, send_sem, recv_sem, device, is_self):
        self.send(source, target, send_sem, recv_sem, device, jnp.logical_not(is_self))
        pl.when(is_self)(pltpu.make_async_copy(source, target, recv_sem).start)

    def landed(self, target, recv_sem):
        pltpu.make_async_copy(target, target, recv_sem).wait()

    def since(self, mark):
        taken, self.open = self.open[mark:], self.open[:mark]
        return taken

    def finish(self, sends):
        for copy, only in sends:
            if only is None:
                copy.wait_send()
            else:
                pl.when(only)(copy.wait_send)

    def close(self):
        self.finish(self.since(0))


def rows_out(mv, buf, block_rows, chunk, send_sem, recv_sem):
    pc = mv.place
    size = block_rows // recv_sem.shape[1]
    part = buf.at[span(pc.rank * block_rows + chunk * size, size)]
    for j in range(1, pc.half):
        other = pc.at(pc.q, pc.c, pc.h, pc.along(j))
        mv.send(part, part, send_sem.at[chunk, j], recv_sem.at[pc.rank, chunk], other)
    mv.send(part, part, send_sem.at[chunk, 0], recv_sem.at[pc.rank, chunk], pc.beside())


def rows_pass(mv, buf, block_rows, j, chunk, pass_sem, recv_sem):
    pc = mv.place
    size = block_rows // recv_sem.shape[1]
    block = pc.c * pc.half + pc.along(j)
    part = buf.at[span(block * block_rows + chunk * size, size)]
    mv.landed(part, recv_sem.at[block, chunk])
    mv.send(part, part, pass_sem.at[chunk, j], recv_sem.at[block, chunk], pc.beside())


def rows_in(mv, buf, block_rows, j, chunk, recv_sem):
    pc = mv.place
    size = block_rows // recv_sem.shape[1]
    block = (1 - pc.c) * pc.half + pc.along(j)
    part = buf.at[span(block * block_rows + chunk * size, size)]
    mv.landed(part, recv_sem.at[block, chunk])


def weights_pass(mv, size, dest, cols, seg, recv_sem, pass_sem, far_sem):
    pc = mv.place
    for c in range(2):
        mv.landed(dest.at[span((2 * pc.q + c) * size, size), cols], recv_sem.at[seg, c])
    both = dest.at[span(2 * pc.q * size, 2 * size), cols]
    if pc.quads == 4:
        for j, quad in enumerate(pc.quad_pair()[:2]):
            mv.send(both, both, pass_sem.at[seg, j], far_sem.at[seg, j], pc.in_quad(quad))
        return
    for j in range(1, pc.quads):
        other = pc.in_quad(pc.across(j))
        mv.send(both, both, pass_sem.at[seg, j - 1], far_sem.at[seg, pc.quads - j - 1], other)


def weights_relay(mv, size, dest, cols, seg, pass_sem, far_sem):
    pc = mv.place
    if pc.quads != 4:
        return
    quads = pc.quad_pair()
    for j in range(2):
        mv.landed(dest.at[span(2 * quads[j] * size, 2 * size), cols], far_sem.at[seg, j])
        part = dest.at[span((2 * quads[j] + j) * size, size), cols]
        mv.send(part, part, pass_sem.at[seg, 2 + j], far_sem.at[seg, 2 + j], pc.in_quad(quads[1 - j]))


def weights_in(mv, size, dest, cols, seg, far_sem):
    pc = mv.place
    if pc.quads == 4:
        for j in range(2):
            part = dest.at[span((2 * pc.quad_pair()[2] + j) * size, size), cols]
            mv.landed(part, far_sem.at[seg, 2 + j])
        return
    for j in range(1, pc.quads):
        part = dest.at[span(2 * pc.across(j) * size, 2 * size), cols]
        mv.landed(part, far_sem.at[seg, j - 1])


def over_tiles(width, body, most=256):
    tile = min(most, width)

    def step(i, carry):
        body(span(i * tile, tile))
        return carry

    lax.fori_loop(0, width // tile, step, 0)


def reduce_rows(mv, s, sems, own, width, partial):
    pc = mv.place
    size = own // CHUNKS
    send_a, recv_a, send_z, recv_z = sems
    order = list(range(1, pc.half)) + [0]
    mark = len(mv.open)
    for j in order:
        block = (1 - pc.c) * pc.half + pc.along(j)

        def give(tile, j=j, block=block):
            s.core_out[j, :, tile] = partial(block, tile).astype(jnp.bfloat16)

        over_tiles(width, give)
        mv.send(s.core_out.at[j], s.core_in.at[j], send_a.at[j], recv_a.at[j], pc.beside())
    for j in order:
        block = pc.c * pc.half + pc.along(j)
        mv.landed(s.core_in.at[j], recv_a.at[j])
        if j:

            def add(tile, j=j, block=block):
                total = partial(block, tile) + s.core_in[j, :, tile].astype(jnp.float32)
                s.chip_out[j - 1, :, tile] = total.astype(jnp.bfloat16)

            over_tiles(width, add)
            other = pc.at(pc.q, pc.c, pc.h, pc.along(j))
            for k in range(CHUNKS):
                rows = pl.ds(k * size, size)
                mv.send(
                    s.chip_out.at[j - 1, rows],
                    s.chip_in.at[pc.half - j - 1, rows],
                    send_z.at[j, k],
                    recv_z.at[pc.half - j, k],
                    other,
                )
        else:

            def hold(tile, block=block):
                total = partial(block, tile) + s.core_in[0, :, tile].astype(jnp.float32)
                s.held[:, tile] = total

            over_tiles(width, hold)
    return mv.since(mark)


def reduced_chunk(mv, s, sems, own, k):
    pc = mv.place
    size = own // CHUNKS
    rows = pl.ds(k * size, size)
    total = s.held[rows, :]
    for j in range(1, pc.half):
        mv.landed(s.chip_in.at[j - 1, rows], sems[3].at[j, k])
        total = total + s.chip_in[j - 1, rows, :].astype(jnp.float32)
    return total


def in_order(mv, buf, own, pass_sem, recv_sem, work, between=None):
    pc = mv.place
    for j in range(pc.half):
        if j:
            for k in range(recv_sem.shape[1]):
                rows_pass(mv, buf, own, j, k, pass_sem, recv_sem)
        work(pc.c * pc.half + pc.along(j))
        for k in range(recv_sem.shape[1]):
            rows_in(mv, buf, own, j, k, recv_sem)
        work((1 - pc.c) * pc.half + pc.along(j))
        if j == 0 and between is not None:
            between()


def to_group(mv, own, source, target, send_sem, recv_sem):
    pc = mv.place
    size = pc.tensor_size
    for j in range(1, size):
        rank = lax.rem(pc.rank + j, size)
        other = pc.at(pc.q, lax.div(rank, pc.half), pc.h, lax.rem(rank, pc.half))
        mv.send(source(rank), target, send_sem.at[j], recv_sem.at[size - j], other)


def grad_out(mv, s, shard, start, width, left, right, seg):
    pc = mv.place

    def rows_of(quad):
        return span(2 * shard * quad, 2 * shard)

    def fill_rows(rows):
        def fill(tile):
            tile_at = pl.ds(pl.multiple_of(start + tile.start, tile.size), tile.size)
            s.grads[rows, tile_at] = dense_tn(left(rows), right(tile)).astype(jnp.bfloat16)

        over_tiles(width, fill)

    if pc.quads == 4:
        quads = pc.quad_pair()
        fill_rows(rows_of(quads[2]))
        for way in range(2):
            cols = pl.ds(start + way * (width // 2), width // 2)
            fill_rows(rows_of(quads[way]))
            for slot, quad in ((1, quads[2]), (0, quads[way])):
                mv.send(
                    s.grads.at[rows_of(quad), cols],
                    s.grads_in.at[slot, :, cols],
                    s.grad_send.at[seg, 2 * way + slot],
                    s.grad_recv.at[seg, 2 * way + slot],
                    pc.in_quad(quads[way]),
                )
        fill_rows(rows_of(pc.q))
        return
    cols = pl.ds(start, width)
    for at in range(0, s.grads.shape[0], 128):
        fill_rows(pl.ds(at, 128))
    for j in range(1, pc.quads):
        quad = pc.across(j)
        mv.send(
            s.grads.at[rows_of(quad), cols],
            s.grads_in.at[pc.quads - j - 1, :, cols],
            s.grad_send.at[seg, j],
            s.grad_recv.at[seg, pc.quads - j],
            pc.in_quad(quad),
        )


def grad_pass(mv, s, shard, start, width, seg):
    pc = mv.place
    if pc.quads != 4:
        return
    quads = pc.quad_pair()
    for way in range(2):
        at = start + way * (width // 2)
        cols = pl.ds(at, width // 2)
        other = quads[1 - way]
        rows = span(2 * shard * other, 2 * shard)
        mv.landed(s.grads_in.at[1, :, cols], s.grad_recv.at[seg, 2 * way + 1])

        def add(tile, at=at, rows=rows):
            tile_at = pl.ds(pl.multiple_of(at + tile.start, 128), tile.size)
            value = s.grads[rows, tile_at].astype(jnp.float32) + s.grads_in[1, :, tile_at].astype(jnp.float32)
            s.grads[rows, tile_at] = value.astype(jnp.bfloat16)

        over_tiles(width // 2, add, 128)
        mv.send(
            s.grads.at[rows, cols],
            s.grads_in.at[2, :, cols],
            s.grad_send.at[seg, 4 + way],
            s.grad_recv.at[seg, 4 + way],
            pc.in_quad(other),
        )


def grad_sum(mv, s, shard, start, width, seg, result):
    pc = mv.place
    cols = pl.ds(start, width)
    if pc.quads == 4:
        for way in range(2):
            part = pl.ds(start + way * (width // 2), width // 2)
            mv.landed(s.grads_in.at[0, :, part], s.grad_recv.at[seg, 2 * way])
            mv.landed(s.grads_in.at[2, :, part], s.grad_recv.at[seg, 4 + way])
        slots = (0, 2)
    else:
        for j in range(1, pc.quads):
            mv.landed(s.grads_in.at[j - 1, :, cols], s.grad_recv.at[seg, j])
        slots = tuple(range(pc.quads - 1))

    def total(tile):
        tile_at = pl.ds(pl.multiple_of(start + tile.start, tile.size), tile.size)
        value = s.grads[span(2 * shard * pc.q, 2 * shard), tile_at].astype(jnp.float32)
        for slot in slots:
            value = value + s.grads_in[slot, :, tile_at].astype(jnp.float32)
        s.grads_out[:, tile_at] = value.astype(jnp.bfloat16)

    over_tiles(width, total)
    for core in range(2):
        mv.keep_or_send(
            s.grads_out.at[pl.ds(core * shard, shard), cols],
            result.at[pc.h, :, cols],
            s.owner_send.at[seg, core],
            s.owner_recv.at[seg, pc.h],
            pc.at(pc.q, core, pc.c, pc.l),
            jnp.logical_and(pc.stays, pc.c == core),
        )


def layer_kernel(names, *refs):
    by_name = dict(zip(names, refs))
    s = types.SimpleNamespace(**by_name)
    sems_ra = (s.ra_send_a, s.ra_recv_a, s.ra_send_z, s.ra_recv_z)
    sems_rb = (s.rb_send_a, s.rb_recv_a, s.rb_send_z, s.rb_recv_z)
    sems_rc = (s.rc_send_a, s.rc_recv_a, s.rc_send_z, s.rc_recv_z)
    pc = Place()
    mv = Mover(pc)
    seq, wide = s.seq, s.wide
    own = s.x.shape[0]
    size = own // CHUNKS
    total_rows, width = seq.shape
    heads = wide.shape[1]
    hidden = s.inner.shape[1]
    shard = s.key_part.shape[0]
    group = pc.tensor_size
    pairs = heads // PAIR
    mine = span(pc.rank * own, own)
    vec, sums = s.vec, s.sums
    f32 = jnp.float32
    inner, hid_cols, head_part = s.inner, pl.ds(0, hidden), pl.ds(0, heads)
    scale = HEAD_DIM ** (-0.5)

    def block_rows(block):
        return span(block * own, own)

    def own_chunk(k):
        return span(pc.rank * own + k * size, size)

    def stack(buf, part):
        return buf.at[pl.ds(part * width, width)]

    def stacked(part, tile):
        return pl.ds(pl.multiple_of(part * width + tile.start, tile.size), tile.size)

    new_rank = pc.h * pc.half + pc.l
    new_out = s.out_all.at[span(new_rank * width, width)]
    my_out = s.out_all.at[span(pc.rank * width, width)]
    parts = (
        (s.out_turned, new_out, my_out, pl.ds(0, heads)),
        (s.inner_part, stack(inner, 0), stack(inner, 0), hid_cols),
        (s.outer_turned, stack(inner, 1), stack(inner, 1), hid_cols),
        (s.query_part, stack(wide, 0), stack(wide, 0), head_part),
        (s.key_part, stack(wide, 1), stack(wide, 1), head_part),
        (s.value_part, stack(wide, 2), stack(wide, 2), head_part),
    )
    attn_parts = (3, 4, 5)

    def start_weight(seg):
        source, target, _, cols = parts[seg]
        place = span((2 * pc.q + pc.c) * shard, shard)
        for half in range(2):
            mv.keep_or_send(
                source,
                target.at[place, cols],
                s.w_send.at[seg, half],
                s.w_recv.at[seg, pc.c],
                pc.at(pc.q, pc.h, half, pc.l),
                jnp.logical_and(pc.stays, pc.h == half),
            )

    def pass_weight(seg):
        weights_pass(mv, shard, parts[seg][2], parts[seg][3], seg, s.w_recv, s.w_pass, s.w_far)

    def relay_weight(seg):
        weights_relay(mv, shard, parts[seg][2], parts[seg][3], seg, s.w_pass, s.w_far)

    def end_weight(seg):
        weights_in(mv, shard, parts[seg][2], parts[seg][3], seg, s.w_far)

    pc.greet()
    column_size = 2 * group
    first = own // FIRST_CHUNKS
    every = s.every
    spot = (2 * pc.q + pc.c) * group + pc.h * pc.half + pc.l
    keep = pltpu.make_async_copy(s.vectors, every.at[spot], s.v_recv.at[0])
    keep.start()
    for j in range(1, column_size):
        mv.send(s.vectors, every.at[spot], s.v_send.at[j], s.v_recv.at[column_size - j], pc.column_peer(j)[1])
    for seg in attn_parts:
        start_weight(seg)
    s.out_turned[...] = jnp.transpose(s.out_part[...])
    s.outer_turned[...] = jnp.transpose(s.outer_part[...])
    sums[...] = jnp.zeros_like(sums)
    keep.wait()
    for j in range(1, column_size):
        mv.landed(every.at[spot], s.v_recv.at[j])
    column = every.at[span(2 * pc.q * group, column_size)]
    for j in range(1, pc.quads):
        mv.send(column, column, s.v_pass.at[j], s.v_far.at[pc.quads - j], pc.in_quad(pc.across(j)))
    for seg in attn_parts:
        pass_weight(seg)
    for k in range(FIRST_CHUNKS):
        mv.keep_or_send(
            s.x.at[pl.ds(k * first, first)],
            seq.at[span(new_rank * own + k * first, first)],
            s.swap_send.at[k],
            s.swap_recv.at[k],
            pc.swapped(),
            pc.stays,
        )
    start_weight(0)
    for j in range(1, pc.quads):
        mv.landed(column, s.v_far.at[j])
    piece = width // (pc.dp_size * group)
    vec[...] = jnp.zeros_like(vec)
    for i in range(pc.dp_size * group):
        vec[0:6, i * piece : (i + 1) * piece] = every[i, 0:6, 0:piece]
    qv_piece, in_piece = heads // pc.dp_size, hidden // pc.dp_size
    for i in range(pc.dp_size):
        held = every[i * group + pc.rank]
        for part in range(2):
            vec[6:7, part * heads + i * qv_piece : part * heads + (i + 1) * qv_piece] = (
                held[6:7, part * qv_piece : (part + 1) * qv_piece]
            )
        vec[7:8, i * in_piece : (i + 1) * in_piece] = held[7:8, 0:in_piece]
    length = every[(2 * pc.q + pc.h) * group][6:7, 127:128]
    for k in range(FIRST_CHUNKS):
        mv.landed(seq.at[span(pc.rank * own + k * first, first)], s.swap_recv.at[k])
        rows_out(mv, seq, own, k, s.row_send, s.row_recv)
        if k == FIRST_CHUNKS - 2:
            for seg in attn_parts:
                relay_weight(seg)
    pass_weight(0)
    start_weight(1)
    for seg in attn_parts:
        end_weight(seg)
    relay_weight(0)

    qkv = s.qkv

    def project(block):
        rows = block_rows(block)
        query = (dense(seq[rows, :], wide[0:width, :]) + vec[6:7, 0:heads]).astype(jnp.bfloat16)
        qkv[rows, 0:heads] = (query.astype(f32) * scale).astype(jnp.bfloat16)
        qkv[rows, heads : 2 * heads] = dense(seq[rows, :], wide[width : 2 * width, :]).astype(jnp.bfloat16)
        value = dense(seq[rows, :], wide[2 * width : 3 * width, :]) + vec[6:7, heads : 2 * heads]
        qkv[rows, 2 * heads : 3 * heads] = value.astype(jnp.bfloat16)

    in_order(mv, seq, own, s.row_pass, s.row_recv, project)
    end_weight(0)
    for k in range(CHUNKS):
        rows_out(mv, s.out_all, width, k, s.out_send, s.out_recv)

    step_rows = min(256, total_rows)
    spot = lax.broadcasted_iota(jnp.int32, (1, total_rows), 1).astype(f32)
    bias = jnp.where(spot < length, 0.0, -jnp.inf).astype(f32)

    def head_cols(pair, head, part):
        start = part * heads + pair * PAIR + head * HEAD_DIM
        return slice(start, start + HEAD_DIM)

    for pair in range(pairs):

        def attend(i, carry, pair=pair):
            rows = span(i * step_rows, step_rows)
            found = []
            for head in range(2):
                scores = dense_nt(qkv[rows, head_cols(pair, head, 0)], qkv[:, head_cols(pair, head, 1)]) + bias
                top = jnp.max(scores, axis=-1, keepdims=True)
                grown = jnp.exp(scores - top)
                total = jnp.sum(grown, axis=-1, keepdims=True)
                probs = (grown * (1.0 / total)).astype(jnp.bfloat16)
                lane = 2 * pair + head
                s.log_total[rows, lane : lane + 1] = top + jnp.log(total)
                found.append(dense(probs, qkv[:, head_cols(pair, head, 2)]))
            s.ctx[rows, pair * PAIR : (pair + 1) * PAIR] = jnp.concatenate(found, axis=1).astype(jnp.bfloat16)
            return carry

        lax.fori_loop(0, total_rows // step_rows, attend, 0)
        place = span(pc.rank * heads + pair * PAIR, PAIR)
        pair_cols = pl.ds(pair * PAIR, PAIR)
        to_group(
            mv, own,
            lambda rank, cols=pair_cols: s.ctx.at[span(rank * own, own), cols],
            s.own_ctx.at[:, place],
            s.ctx_send.at[pair], s.ctx_recv.at[pair],
        )
        s.own_ctx[:, place] = s.ctx[mine, pair_cols]
        if pair == 0:
            for j in range(1, pc.half):
                for k in range(CHUNKS):
                    rows_pass(mv, s.out_all, width, j, k, s.out_pass, s.out_recv)
            pass_weight(1)
            start_weight(2)
    mv.keep_or_send(s.cot, s.cot_in, s.cot_send.at[0], s.cot_recv.at[0], pc.swapped(), pc.stays)
    for pair in range(pairs):
        for j in range(1, group):
            mv.landed(s.own_ctx.at[:, pl.ds(0, PAIR)], s.ctx_recv.at[pair, j])
    relay_weight(1)
    pass_weight(2)
    for j in range(pc.half):
        for k in range(CHUNKS):
            rows_in(mv, s.out_all, width, j, k, s.out_recv)

    for k in range(CHUNKS):
        rows = pl.ds(k * size, size)
        total = seq[own_chunk(k), :].astype(f32) + vec[0:1, :]
        for t in range(group):
            total = total + dense_nt(
                s.own_ctx[rows, t * heads : (t + 1) * heads], s.out_all[t * width : (t + 1) * width, :]
            )
        s.resid[rows, :] = total
        normed, _ = norm_parts(total)
        middle = normed * vec[1:2, :] + vec[2:3, :]
        s.middle[rows, :] = middle
        s.mid_rows[own_chunk(k), :] = middle.astype(jnp.bfloat16)
        rows_out(mv, s.mid_rows, own, k, s.mid_send, s.mid_recv)

    end_weight(1)

    def expand(block):
        rows = block_rows(block)

        def one(tile):
            pre = dense(s.mid_rows[rows, :], inner[0:width, tile]) + vec[7:8, tile]
            cdf = 0.5 * (1.0 + lax.erf(pre * inv_root2))
            s.hid[rows, tile] = (pre * cdf).astype(jnp.bfloat16)
            s.slope[rows, tile] = cdf + pre * inv_root2pi * jnp.exp(-0.5 * pre * pre)

        over_tiles(hidden, one)

    in_order(mv, s.mid_rows, own, s.mid_pass, s.mid_recv, expand, lambda: relay_weight(2))
    end_weight(2)
    sent_ra = reduce_rows(
        mv, s, sems_ra, own, width,
        lambda block, tile: dense_nt(s.hid[block_rows(block), :], inner[stacked(1, tile), :]),
    )
    mv.landed(s.cot_in, s.cot_recv.at[0])
    for k in range(CHUNKS):
        rows = pl.ds(k * size, size)
        total = s.middle[rows, :] + reduced_chunk(mv, s, sems_ra, own, k) + vec[3:4, :]
        normed, inverse = norm_parts(total)
        up = s.cot_in[rows, :].astype(f32)
        d_resid = norm_back(normed, inverse, vec[4:5, :], up)
        s.d_resid[rows, :] = d_resid
        s.ffn_rows[own_chunk(k), :] = d_resid.astype(jnp.bfloat16)
        rows_out(mv, s.ffn_rows, own, k, s.ffn_send, s.ffn_recv)
        sums[3:4, :] += jnp.sum(d_resid, axis=0, keepdims=True)
        sums[4:5, :] += jnp.sum(up * normed, axis=0, keepdims=True)
        sums[5:6, :] += jnp.sum(up, axis=0, keepdims=True)
        s.out_stage[rows, :] = (normed * vec[4:5, :] + vec[5:6, :]).astype(jnp.bfloat16)

    mv.finish(sent_ra)

    def shrink(block):
        rows = block_rows(block)

        def one(tile):
            d_pre = dense(s.ffn_rows[rows, :], inner[width : 2 * width, tile]) * s.slope[rows, tile]
            sums[7:8, tile] += jnp.sum(d_pre, axis=0, keepdims=True)
            s.d_pre[rows, tile] = d_pre.astype(jnp.bfloat16)

        over_tiles(hidden, one)

    in_order(mv, s.ffn_rows, own, s.ffn_pass, s.ffn_recv, shrink)
    sent_rb = reduce_rows(
        mv, s, sems_rb, own, width,
        lambda block, tile: dense_nt(s.d_pre[block_rows(block), :], inner[tile, :]),
    )
    at_out, at_in, at_outer = 3 * heads, 4 * heads, 4 * heads + hidden
    grad_out(
        mv, s, shard, at_outer, hidden,
        lambda rows: s.ffn_rows[:, rows], lambda tile: s.hid[:, tile], 0,
    )
    grad_out(
        mv, s, shard, at_in, hidden,
        lambda rows: s.mid_rows[:, rows], lambda tile: s.d_pre[:, tile], 1,
    )
    for k in range(CHUNKS):
        rows = pl.ds(k * size, size)
        up = reduced_chunk(mv, s, sems_rb, own, k) + s.d_resid[rows, :]
        normed, inverse = norm_parts(s.resid[rows, :])
        d_resid = norm_back(normed, inverse, vec[1:2, :], up)
        s.d_resid[rows, :] = d_resid
        s.attn_rows[own_chunk(k), :] = d_resid.astype(jnp.bfloat16)
        sums[0:1, :] += jnp.sum(d_resid, axis=0, keepdims=True)
        sums[1:2, :] += jnp.sum(up * normed, axis=0, keepdims=True)
        sums[2:3, :] += jnp.sum(up, axis=0, keepdims=True)

    mv.finish(sent_rb)
    for k in range(CHUNKS):
        rows = pl.ds(k * size, size)
        mv.keep_or_send(
            s.out_stage.at[rows], s.block_out.at[rows],
            s.bo_send.at[k], s.bo_recv.at[k], pc.swapped(), pc.stays,
        )

    for t in range(group):
        s.d_ctx_out[t, :, :] = dense(
            s.attn_rows[mine, :], s.out_all[t * width : (t + 1) * width, :]
        ).astype(jnp.bfloat16)
    to_group(
        mv, own,
        lambda rank: s.d_ctx_out.at[rank],
        s.d_ctx.at[mine],
        s.d_ctx_send, s.d_ctx_recv,
    )
    s.d_ctx[mine, :] = s.d_ctx_out[pc.rank, :, :]
    for k in range(CHUNKS):
        rows_out(mv, s.attn_rows, own, k, s.at_send, s.at_recv)
    for j in range(1, group):
        mv.landed(s.d_ctx.at[mine], s.d_ctx_recv.at[j])
    d_qkv = s.d_qkv
    grad_pass(mv, s, shard, at_outer, hidden, 0)
    for pair in range(pairs):
        s.key_sum[...] = jnp.zeros_like(s.key_sum)
        s.value_sum[...] = jnp.zeros_like(s.value_sum)

        def attend_back(i, carry, pair=pair):
            rows = span(i * step_rows, step_rows)
            found = []
            for head in range(2):
                cols = slice(head * HEAD_DIM, (head + 1) * HEAD_DIM)
                lane = 2 * pair + head
                query, key = qkv[rows, head_cols(pair, head, 0)], qkv[:, head_cols(pair, head, 1)]
                grad = s.d_ctx[rows, head_cols(pair, head, 0)]
                scores = dense_nt(query, key) + bias
                probs = jnp.exp(scores - s.log_total[rows, lane : lane + 1])
                d_probs = dense_nt(grad, qkv[:, head_cols(pair, head, 2)])
                within = jnp.sum(probs * d_probs, axis=-1, keepdims=True)
                d_scores = (probs * (d_probs - within)).astype(jnp.bfloat16)
                found.append(dense(d_scores, key) * scale)
                s.value_sum[cols, :] += dense_tn(grad, probs.astype(jnp.bfloat16))
                s.key_sum[cols, :] += dense_tn(query, d_scores)
            d_query = jnp.concatenate(found, axis=1)
            d_qkv[rows, pair * PAIR : (pair + 1) * PAIR] = d_query.astype(jnp.bfloat16)
            sums[6:7, pair * PAIR : (pair + 1) * PAIR] += jnp.sum(d_query, axis=0, keepdims=True)
            return carry

        lax.fori_loop(0, total_rows // step_rows, attend_back, 0)
        at_key = slice(heads + pair * PAIR, heads + (pair + 1) * PAIR)
        at_value = slice(2 * heads + pair * PAIR, 2 * heads + (pair + 1) * PAIR)
        d_qkv[:, at_key] = jnp.transpose(s.key_sum[...]).astype(jnp.bfloat16)
        d_value = jnp.transpose(s.value_sum[...])
        d_qkv[:, at_value] = d_value.astype(jnp.bfloat16)
        sums[6:7, at_key] = jnp.sum(d_value, axis=0, keepdims=True)
        if pair == 0:
            grad_sum(mv, s, shard, at_outer, hidden, 0, s.weight_grads)
            grad_pass(mv, s, shard, at_in, hidden, 1)
            for j in range(1, pc.half):
                for k in range(CHUNKS):
                    rows_pass(mv, s.attn_rows, own, j, k, s.at_pass, s.at_recv)
            for j in range(pc.half):
                for k in range(CHUNKS):
                    rows_in(mv, s.attn_rows, own, j, k, s.at_recv)
            grad_out(
                mv, s, shard, at_out, heads,
                lambda rows: s.attn_rows[:, rows], lambda tile: s.ctx[:, tile], 2,
            )
    slots = s.sum_slots
    slots[pc.column] = sums[...]
    for j in range(1, 2 * group):
        mv.send(
            sums, slots.at[pc.column],
            s.sum_send.at[j], s.sum_recv.at[2 * group - j], pc.column_peer(j)[1],
        )
    grad_out(
        mv, s, shard, 0, 3 * heads,
        lambda rows: seq[:, rows], lambda tile: d_qkv[:, tile], 3,
    )
    sent_rc = reduce_rows(
        mv, s, sems_rc, own, width,
        lambda block, tile: sum(
            dense_nt(d_qkv[block_rows(block), part * heads : (part + 1) * heads], wide[stacked(part, tile), :])
            for part in range(3)
        ),
    )
    grad_sum(mv, s, shard, at_in, hidden, 1, s.weight_grads)
    grad_pass(mv, s, shard, at_out, heads, 2)
    grad_sum(mv, s, shard, at_out, heads, 2, s.weight_grads)
    for k in range(CHUNKS):
        if k == CHUNKS // 2:
            grad_pass(mv, s, shard, 0, 3 * heads, 3)
        rows = pl.ds(k * size, size)
        s.ig_stage[rows, :] = (reduced_chunk(mv, s, sems_rc, own, k) + s.d_resid[rows, :]).astype(jnp.bfloat16)
        mv.keep_or_send(
            s.ig_stage.at[rows], s.input_grad.at[rows],
            s.ig_send.at[k], s.ig_recv.at[k], pc.swapped(), pc.stays,
        )
    mv.finish(sent_rc)
    for j in range(1, 2 * group):
        mv.landed(slots.at[0], s.sum_recv.at[j])
    whole = slots[0]
    for j in range(1, 2 * group):
        whole = whole + slots[j]
    chosen = pc.h * group + pc.l
    biases = slots[chosen] + slots[chosen + pc.half]
    row = lax.broadcasted_iota(jnp.int32, whole.shape, 0)
    summed = jnp.where(row < 6, whole, biases)
    s.sum_stage[...] = summed
    for j in range(1, pc.quads):
        other = pc.at(pc.across(j), pc.c, pc.h, pc.l)
        mv.send(s.sum_stage, s.sum_far.at[pc.quads - j - 1], s.far_send.at[j], s.far_recv.at[pc.quads - j], other)
    for j in range(1, pc.quads):
        mv.landed(s.sum_stage, s.far_recv.at[j])
        summed = summed + s.sum_far[j - 1]
    s.vec_grads[...] = summed
    grad_sum(mv, s, shard, 0, 3 * heads, 3, s.weight_grads)
    for k in range(CHUNKS):
        rows = pl.ds(k * size, size)
        mv.landed(s.block_out.at[rows], s.bo_recv.at[k])
        mv.landed(s.input_grad.at[rows], s.ig_recv.at[k])
    for seg, (start, count) in enumerate(
        ((at_outer, hidden), (at_in, hidden), (at_out, heads), (0, 3 * heads))
    ):
        for h in range(2):
            mv.landed(s.weight_grads.at[h, :, pl.ds(start, count)], s.owner_recv.at[seg, h])
    mv.close()


def run_layer(x, query_part, key_part, value_part, out_part, inner_part, outer_part, vectors, cot):
    dp_size, tensor_size = lax.axis_size("dp"), lax.axis_size("tensor")
    quads, half = dp_size // 2, tensor_size // 2
    own, width = x.shape
    rows = own * tensor_size
    shard, heads = query_part.shape
    hidden = inner_part.shape[1]
    pairs = heads // PAIR
    every = 4 * heads + 2 * hidden
    bf16, f32 = jnp.bfloat16, jnp.float32
    ins = dict(
        x=x, query_part=query_part, key_part=key_part, value_part=value_part, inner_part=inner_part,
        vectors=vectors, cot=cot, out_part=out_part, outer_part=outer_part,
    )
    outs = dict(
        block_out=((own, width), bf16),
        input_grad=((own, width), bf16),
        weight_grads=((2, shard, every), bf16),
        vec_grads=((8, width), f32),
    )
    buffers = dict(
        seq=((rows, width), bf16),
        wide=((3 * width, heads), bf16),
        vec=((8, width), f32),
        every=((dp_size * tensor_size,) + vectors.shape, f32),
        out_turned=((shard, heads), bf16),
        outer_turned=((shard, hidden), bf16),
        inner=((2 * width, hidden), bf16),
        out_all=((tensor_size * width, heads), bf16),
        qkv=((rows, 3 * heads), bf16),
        log_total=((rows, 128), f32),
        ctx=((rows, heads), bf16),
        own_ctx=((own, width), bf16),
        resid=((own, width), f32),
        middle=((own, width), f32),
        d_resid=((own, width), f32),
        held=((own, width), f32),
        mid_rows=((rows, width), bf16),
        slope=((rows, hidden), f32),
        hid=((rows, hidden), bf16),
        ffn_rows=((rows, width), bf16),
        d_pre=((rows, hidden), bf16),
        attn_rows=((rows, width), bf16),
        d_ctx_out=((tensor_size, own, heads), bf16),
        d_ctx=((rows, heads), bf16),
        d_qkv=((rows, 3 * heads), bf16),
        key_sum=((PAIR, rows), f32),
        value_sum=((PAIR, rows), f32),
        core_out=((half, own, width), bf16),
        core_in=((half, own, width), bf16),
        chip_out=((half - 1, own, width), bf16),
        chip_in=((half - 1, own, width), bf16),
        grads=((width, every), bf16),
        grads_in=((quads - 1, 2 * shard, every), bf16),
        grads_out=((2 * shard, every), bf16),
        cot_in=((own, width), bf16),
        out_stage=((own, width), bf16),
        ig_stage=((own, width), bf16),
        sums=((8, width), f32),
        sum_slots=((2 * tensor_size, 8, width), f32),
        sum_stage=((8, width), f32),
        sum_far=((quads - 1, 8, width), f32),
    )
    sems = dict(
        w_send=(6, 2), w_recv=(6, 2), w_pass=(6, quads), w_far=(6, quads),
        swap_send=(FIRST_CHUNKS,), swap_recv=(FIRST_CHUNKS,),
        v_send=(2 * tensor_size,), v_recv=(2 * tensor_size,), v_pass=(quads,), v_far=(quads,),
        cot_send=(1,), cot_recv=(1,),
        ctx_send=(pairs, tensor_size), ctx_recv=(pairs, tensor_size),
        d_ctx_send=(tensor_size,), d_ctx_recv=(tensor_size,),
        bo_send=(CHUNKS,), bo_recv=(CHUNKS,), ig_send=(CHUNKS,), ig_recv=(CHUNKS,),
        grad_send=(4, quads + 2), grad_recv=(4, quads + 2), owner_send=(4, 2), owner_recv=(4, 2),
        sum_send=(2 * tensor_size,), sum_recv=(2 * tensor_size,), far_send=(quads,), far_recv=(quads,),
    )
    for tag in ("row", "out", "mid", "ffn", "at"):
        sems[tag + "_send"] = (CHUNKS, half)
        sems[tag + "_recv"] = (tensor_size, CHUNKS)
        sems[tag + "_pass"] = (CHUNKS, half)
    sems.update(
        row_send=(FIRST_CHUNKS, half), row_recv=(tensor_size, FIRST_CHUNKS), row_pass=(FIRST_CHUNKS, half)
    )
    for tag in ("ra", "rb", "rc"):
        sems[tag + "_send_a"] = (half,)
        sems[tag + "_recv_a"] = (half,)
        sems[tag + "_send_z"] = (half, CHUNKS)
        sems[tag + "_recv_z"] = (half, CHUNKS)
    names = tuple(ins) + tuple(outs) + tuple(buffers) + tuple(sems)
    vmem, anywhere = pl.BlockSpec(memory_space=pltpu.VMEM), pl.BlockSpec(memory_space=pl.ANY)
    return pl.pallas_call(
        functools.partial(layer_kernel, names),
        out_shape=[jax.ShapeDtypeStruct(shape, kind) for shape, kind in outs.values()],
        in_specs=[anywhere] * 7 + [vmem] * 2,
        out_specs=[vmem] * len(outs),
        scratch_shapes=[pltpu.VMEM(shape, kind) for shape, kind in buffers.values()]
        + [pltpu.SemaphoreType.DMA(shape) for shape in sems.values()],
        compiler_params=pltpu.CompilerParams(
            collective_id=0, has_side_effects=True, vmem_limit_bytes=VMEM_LIMIT
        ),
        name="layer",
    )(*ins.values())


def finish_kernel(cuts, block_ref, input_ref, grads_ref, out_block, out_input, *out_grads):
    out_block[...] = block_ref[...]
    out_input[...] = input_ref[...].astype(jnp.float32)
    for i, out in enumerate(out_grads):
        cols = slice(cuts[i], cuts[i + 1])
        total = grads_ref[0, :, cols].astype(jnp.float32) + grads_ref[1, :, cols].astype(jnp.float32)
        out[...] = total if out.shape == total.shape else jnp.transpose(total)


def finish(block_out, input_grad, weight_grads, shapes):
    cuts = [0]
    for shape, turned in shapes:
        cuts.append(cuts[-1] + (shape[0] if turned else shape[1]))
    f32 = jnp.float32
    return pl.pallas_call(
        functools.partial(finish_kernel, cuts),
        out_shape=[
            jax.ShapeDtypeStruct(block_out.shape, block_out.dtype),
            jax.ShapeDtypeStruct(input_grad.shape, f32),
        ]
        + [jax.ShapeDtypeStruct(shape, f32) for shape, _ in shapes],
        compiler_params=pltpu.CompilerParams(vmem_limit_bytes=32 << 20),
        name="finish",
    )(block_out, input_grad, weight_grads)


def per_device(
    block_input,
    lengths,
    query_weight,
    key_weight,
    value_weight,
    query_bias,
    value_bias,
    output_weight,
    output_bias,
    first_gain,
    first_shift,
    inner_weight,
    inner_bias,
    outer_weight,
    outer_bias,
    second_gain,
    second_shift,
    cotangent,
):
    f32 = jnp.float32
    dp_size, tensor_size = lax.axis_size("dp"), lax.axis_size("tensor")
    dp, tensor = lax.axis_index("dp"), lax.axis_index("tensor")

    features = (output_bias, first_gain, first_shift, outer_bias, second_gain, second_shift)
    biases = (query_bias, value_bias, inner_bias)
    def lanes(row):
        return jnp.pad(row, ((0, 0), (0, 128 - row.shape[1])))

    query_bias, value_bias, inner_bias = (bias.astype(f32)[None] for bias in biases)
    mixed = jnp.concatenate([query_bias, value_bias], axis=1)
    length = jnp.broadcast_to(lengths.astype(f32)[None], (1, 128 - mixed.shape[1]))
    vectors = jnp.concatenate(
        [lanes(jnp.stack(features)), jnp.concatenate([mixed, length], axis=1), lanes(inner_bias)]
    )
    block_out, input_grad, weight_grads, vec_grads = run_layer(
        block_input, query_weight, key_weight, value_weight, output_weight, inner_weight, outer_weight,
        vectors, cotangent,
    )

    width = block_input.shape[1]
    heads, hidden = query_weight.shape[1], inner_weight.shape[1]
    block_out, input_grad, *pieces = finish(
        block_out, input_grad, weight_grads,
        (
            (query_weight.shape, False),
            (key_weight.shape, False),
            (value_weight.shape, False),
            (output_weight.shape, True),
            (inner_weight.shape, False),
            (outer_weight.shape, True),
        ),
    )
    piece = width // (dp_size * tensor_size)
    mine = lax.dynamic_slice_in_dim(vec_grads, (dp * tensor_size + tensor) * piece, piece, axis=1)

    def bias_piece(row, start, count):
        size = count // dp_size
        return lax.dynamic_slice(vec_grads, (row, start + dp * size), (1, size))[0]

    return (
        block_out,
        input_grad,
        pieces[0],
        pieces[1],
        pieces[2],
        bias_piece(6, 0, heads),
        bias_piece(6, heads, heads),
        pieces[3],
        mine[0],
        mine[1],
        mine[2],
        pieces[4],
        bias_piece(7, 0, hidden),
        pieces[5],
        mine[3],
        mine[4],
        mine[5],
    )


def solution(mesh):
    return jax.shard_map(
        per_device,
        mesh=mesh,
        in_specs=(
            P(("dp", "tensor"), None),
            P("dp"),
            P("dp", "tensor"),
            P("dp", "tensor"),
            P("dp", "tensor"),
            P(("tensor", "dp")),
            P(("tensor", "dp")),
            P("tensor", "dp"),
            P(("dp", "tensor")),
            P(("dp", "tensor")),
            P(("dp", "tensor")),
            P("dp", "tensor"),
            P(("tensor", "dp")),
            P("tensor", "dp"),
            P(("dp", "tensor")),
            P(("dp", "tensor")),
            P(("dp", "tensor")),
            P(("dp", "tensor"), None),
        ),
        out_specs=(
            P(("dp", "tensor"), None),
            P(("dp", "tensor"), None),
            P("dp", "tensor"),
            P("dp", "tensor"),
            P("dp", "tensor"),
            P(("tensor", "dp")),
            P(("tensor", "dp")),
            P("tensor", "dp"),
            P(("dp", "tensor")),
            P(("dp", "tensor")),
            P(("dp", "tensor")),
            P("dp", "tensor"),
            P(("tensor", "dp")),
            P("tensor", "dp"),
            P(("dp", "tensor")),
            P(("dp", "tensor")),
            P(("dp", "tensor")),
        ),
        check_vma=False,
    )
```
